32 devices in a mesh: groups: 2 (over y), seq: 4 (over z), head: 2 (over x), sub: 2 (over core).
Axes of the slice: x: 2, y: 2, z: 4, core: 2. Of those that a mesh axis runs over, the one named last changes fastest.
Arguments:
- wave_pieces: float32 [8, 2, 2, 64, 3072], P(('groups', 'seq'), 'head', 'sub'), parts along dimension 0, may hold values from -6 to 6
- piece_target: int32 [8, 2, 2, 64], P(('groups', 'seq'), 'head', 'sub'), parts along dimension 0, may hold values from -1 to 127, as said below
- utt_lengths: int32 [8], P('groups'), parts along dimension 0, may hold values from 1 to 1088, 2176 in all
- sub_weight: bfloat16 [512, 1536], P(None, 'head'), may hold values from -2 to 2
- sub_bias: bfloat16 [1536], P('head'), may hold values from -4 to 4
- norm_gain: float32 [1536], replicated, may hold values from 0.1 to 1.9
- qkv_weight: bfloat16 [1536, 3, 1536], P(None, None, 'head'), may hold values from -0.21875 to 0.21875
- rel_bias: float32 [24, 543], P('head'), may hold values from -4 to 250
Outputs:
- context: bfloat16 [4352, 1536], P(('groups', 'seq', 'sub'), 'head'), parts along dimension 0
The draws below stay inside these ranges and needn't reach their ends.
There are 2 independent parts, one for each index of `groups`. The reference program is written for one: setup_inputs(seed, part) draws one part's arguments, and reference() takes and returns one part's arrays. A program takes and returns all parts, laid end to end along the dimension named above; an argument that names none is the same for every part. Nothing has to cross between parts.
Inputs may be any that keep to these rules, and one draw needn't show every extreme that they name: `piece_target`: each value is -1 (an empty slot) or s * 32 + p, naming piece p of seq index s for the loader's own head and sub indices. Every piece of every eighth is named by exactly one slot of a loader with the same head and sub indices. A loader names at most 16 pieces of one seq index; in every draw some loaders name exactly 16 pieces of every seq index, so that all their slots are full.
All inputs are finite; a program needn't handle non-finite values.
Results may differ from the reference program's by a relative error of at most 0.006.
Values may be sent and summed in bfloat16 or wider, within the bound.
A program may use at most 64 MiB of HBM per device.

```python
import math
import jax
import jax.numpy as jnp
import numpy as np
from jax import lax

D = 1536
HEADS = 24
HDIM = 64
MEL = 128
NFFT = 512
HOP = 160
FP = 17
CH = 136
PE = 32
PL = 3072
BINS = 257
CAP = 16
LOAD = 64
HEAVY = 1
HALF_TOK = 272
TOKENS = 2176
UTTS = 4
UTT_MOST = 1088
N_SEQ = 4
N_HEAD = 2
N_SUB = 2


def draw_wave_pieces(key, part):
    key_noise, key_gain = jax.random.split(jax.random.fold_in(key, 3))
    shape = (N_SEQ, N_HEAD, N_SUB, LOAD, PL)
    gains = jnp.exp(jax.random.uniform(key_gain, (N_SEQ, N_HEAD, N_SUB, LOAD, 1), jnp.float32, math.log(0.1), 0.0))
    noise = jnp.clip(jax.random.normal(key_noise, shape, jnp.float32), -6.0, 6.0)
    return (noise * gains).astype(jnp.float32)


def column_plan(key):
    key_heavy, key_extra, key_place, key_order = jax.random.split(key, 4)
    heavy_rank = jax.random.permutation(key_heavy, N_SEQ)
    is_heavy = heavy_rank < HEAVY
    light_total = PE - HEAVY * CAP
    light_loaders = N_SEQ - HEAVY
    light_base = light_total // light_loaders
    light_extra = light_total % light_loaders
    priority = jax.vmap(lambda sub_key: jax.random.permutation(sub_key, N_SEQ))(jax.random.split(key_extra, N_SEQ))
    ahead = (priority[:, None, :] < priority[:, :, None]) & jnp.logical_not(is_heavy)[None, None, :]
    light_rank = jnp.sum(ahead.astype(jnp.int32), axis=2)
    counts = jnp.where(is_heavy[None, :], CAP, light_base + (light_rank < light_extra).astype(jnp.int32))
    offsets = jnp.cumsum(counts, axis=1) - counts
    placement = jax.vmap(lambda sub_key: jax.random.permutation(sub_key, PE))(jax.random.split(key_place, N_SEQ))
    slot_number = jnp.arange(LOAD)
    slot_shard = slot_number // CAP
    slot_rank = slot_number % CAP
    live = slot_rank[None, :] < jnp.transpose(counts)[:, slot_shard]
    order_index = jnp.minimum(jnp.transpose(offsets)[:, slot_shard] + slot_rank[None, :], PE - 1)
    position = placement[slot_shard[None, :], order_index]
    targets = jnp.where(live, slot_shard[None, :] * PE + position, -1)
    shuffles = jax.vmap(lambda sub_key: jax.random.permutation(sub_key, LOAD))(jax.random.split(key_order, N_SEQ))
    return jnp.take_along_axis(targets, shuffles, axis=1).astype(jnp.int32)


def draw_piece_target(key, part):
    column_keys = jax.random.split(jax.random.fold_in(key, 11), N_HEAD * N_SUB)
    per_column = jax.vmap(column_plan)(column_keys)
    return jnp.transpose(per_column.reshape(N_HEAD, N_SUB, N_SEQ, LOAD), (2, 0, 1, 3)).astype(jnp.int32)


def draw_sub_weight(key, part):
    key_values, key_scale = jax.random.split(jax.random.fold_in(key, 7))
    column_scale = jnp.exp(jax.random.uniform(key_scale, (1, D), jnp.float32, math.log(0.3), math.log(3.0)))
    values = jnp.clip(jax.random.normal(key_values, (4 * MEL, D), jnp.float32), -4.0, 4.0)
    return (values * column_scale * (1.0 / math.sqrt(4 * MEL))).astype(jnp.bfloat16)


def draw_rel_bias(key, part):
    width = 4 * CH - 1
    key_values = jax.random.fold_in(key, 5)
    values = jnp.clip(jax.random.normal(key_values, (HEADS, width), jnp.float32), -4.0, 4.0)
    return values.astype(jnp.float32)


def shard_levels(own_key, shape, shards, low, high):
    def one(axis_at, blocks):
        heights = jax.random.uniform(jax.random.fold_in(jax.random.fold_in(own_key, 6), axis_at), (blocks,), jnp.float32, low / len(shards), high / len(shards))
        return jnp.repeat(jnp.exp(heights), shape[axis_at] // blocks).reshape((-1,) + (1,) * (len(shape) - axis_at - 1))

    level = one(*shards[0])
    for cut in shards[1:]:
        level = level * one(*cut)
    return level


def length_profile(amount, total, limit, slope):
    portions = [(1 << 20) // math.isqrt(standing ** slope) + 1 for standing in range(2, amount + 1)]
    rest, given = total - limit - (amount - 1), [1] * (amount - 1)
    while rest > 0:
        free = [i for i in range(amount - 1) if given[i] < limit]
        pool, remaining = sum([portions[i] for i in free]), rest
        for i in free:
            more = min(limit - given[i], max(1, remaining * portions[i] // pool), rest)
            given[i] = given[i] + more
            rest = rest - more
    return np.array([limit] + given)


def ragged(rng, count, total, bound, lean):
    if count == 2:
        one = jax.random.randint(rng, (), max(1, total - bound), min(bound, total - 1) + 1)
        return jnp.stack([one, total - one])
    sizes = jnp.asarray(length_profile(count, total, bound, lean), jnp.int32)
    twos = (count - 1) // 2
    source_of, taker = sizes[1:1 + 2 * twos:2], sizes[2:2 + 2 * twos:2]
    margin = jnp.minimum(source_of - 1, bound - taker)
    shifted = jax.random.randint(jax.random.fold_in(rng, 1), (twos,), 0, 1 << 20) % (margin + 1)
    sizes = sizes.at[1:1 + 2 * twos:2].set(source_of - shifted).at[2:2 + 2 * twos:2].set(taker + shifted)
    return sizes[jax.random.permutation(jax.random.fold_in(rng, 2), count)]


def normal_values(key, dims, deviation, bound, pieces=(), held_as=jnp.bfloat16):
    array = deviation * jax.random.normal(key, dims, jnp.float32)
    if pieces:
        array = array * shard_levels(key, dims, pieces, -0.22, 0.18)
    return jnp.clip(array, -bound, bound).astype(held_as)


def setup_inputs(seed: int = 0, part: int = 0) -> dict:
    arg_keys = jax.random.split(jax.random.key(seed), 9)
    part_keys = jax.random.split(jax.random.fold_in(arg_keys[8], part), 9)
    wave_pieces = draw_wave_pieces(jax.random.fold_in(jax.random.fold_in(arg_keys[8], part), 71), part)
    piece_target = draw_piece_target(jax.random.fold_in(jax.random.fold_in(arg_keys[8], part), 71), part)
    utt_lengths = ragged(part_keys[2], UTTS, TOKENS, UTT_MOST, 2).astype(jnp.int32)
    sub_weight = draw_sub_weight(jax.random.fold_in(arg_keys[8], 71), part)
    sub_bias = normal_values(arg_keys[4], (D,), 1.0, 4.0, ((0, 2),))
    norm_gain = jnp.clip(1.0 + 0.18 * jax.random.normal(arg_keys[5], (D,), jnp.float32), 0.1, 1.9)
    qkv_weight = normal_values(arg_keys[6], (D, 3, D), (D // 2) ** -0.5, 0.21875, ((2, 2),))
    rel_bias = draw_rel_bias(jax.random.fold_in(arg_keys[8], 71), part)
    return {"wave_pieces": wave_pieces, "piece_target": piece_target, "utt_lengths": utt_lengths, "sub_weight": sub_weight, "sub_bias": sub_bias, "norm_gain": norm_gain, "qkv_weight": qkv_weight, "rel_bias": rel_bias}


SAMPLE_RATE = 16000.0
EPSILON = 1e-05
MASKED = -1e+30

def window_table():
    sample_index = jnp.arange(NFFT).astype(jnp.float32)
    return 0.5 - 0.5 * jnp.cos(2.0 * math.pi / NFFT * sample_index)

def fourier_table():
    sample_index = jnp.arange(NFFT).astype(jnp.int32)[:, None]
    bin_index = jnp.arange(BINS).astype(jnp.int32)[None, :]
    phase = (sample_index * bin_index % NFFT).astype(jnp.float32) * (2.0 * math.pi / NFFT)
    return jnp.concatenate([jnp.cos(phase), jnp.sin(phase)], axis=1)

def mel_table():
    highest = 2595.0 * math.log10(1.0 + SAMPLE_RATE / 2.0 / 700.0)
    points = jnp.arange(MEL + 2).astype(jnp.float32) * (highest / (MEL + 1))
    hertz = 700.0 * (jnp.power(10.0, points / 2595.0) - 1.0)
    centres = jnp.arange(BINS).astype(jnp.float32) * (SAMPLE_RATE / NFFT)
    rising = (centres[:, None] - hertz[None, :-2]) / (hertz[1:-1] - hertz[:-2])[None, :]
    falling = (hertz[None, 2:] - centres[:, None]) / (hertz[2:] - hertz[1:-1])[None, :]
    return jnp.maximum(0.0, jnp.minimum(rising, falling))

def log_mel(piece_rows):
    piece_count = piece_rows.shape[0]
    frames = jnp.stack([piece_rows[:, HOP * frame_index:HOP * frame_index + NFFT] for frame_index in range(FP)], axis=1)
    frames = frames * window_table()[None, None, :]
    spectra = jnp.dot(frames.reshape(piece_count * FP, NFFT), fourier_table(), precision=lax.Precision.HIGHEST)
    power_bins = spectra[:, :BINS] * spectra[:, :BINS] + spectra[:, BINS:] * spectra[:, BINS:]
    energy = jnp.dot(power_bins, mel_table(), precision=lax.Precision.HIGHEST)
    return jnp.log(1.0 + energy).astype(jnp.bfloat16).reshape(piece_count, FP * MEL)

def reference(wave_pieces, piece_target, utt_lengths, sub_weight, sub_bias, norm_gain, qkv_weight, rel_bias):
    column_count = N_HEAD * N_SUB
    slot_rows = jnp.transpose(wave_pieces, (1, 2, 0, 3, 4)).reshape(column_count, N_SEQ * LOAD, PL)
    targets = jnp.transpose(piece_target, (1, 2, 0, 3)).reshape(column_count, N_SEQ * LOAD).astype(jnp.int32)
    targets = jnp.where(targets < 0, N_SEQ * PE, targets).astype(jnp.int32)

    def place(column_rows, slot_goals):
        return jnp.zeros((N_SEQ * PE, PL), jnp.float32).at[slot_goals].set(column_rows.astype(jnp.float32), mode='drop')
    placed = jax.vmap(place)(slot_rows, targets)
    placed = jnp.transpose(placed.reshape(N_HEAD, N_SUB, N_SEQ, PE, PL), (2, 1, 0, 3, 4))

    def shard_mel(shard_pieces):
        return log_mel(shard_pieces.reshape(N_SUB * N_HEAD * PE, PL))
    mel_pieces = lax.map(shard_mel, placed)
    token_rows = mel_pieces.reshape(TOKENS, 4 * MEL)
    features = jax.nn.silu(jnp.dot(token_rows, sub_weight, preferred_element_type=jnp.float32) + sub_bias.astype(jnp.float32)).astype(jnp.bfloat16)

    def project(half_rows):
        values = half_rows.astype(jnp.float32)
        centred = values - lax.optimization_barrier(jnp.mean(values, axis=1, keepdims=True))
        variance = lax.optimization_barrier(jnp.mean(centred * centred, axis=1, keepdims=True))
        normed = (centred * lax.rsqrt(variance + EPSILON) * norm_gain[None, :]).astype(jnp.bfloat16)
        return jnp.dot(normed, qkv_weight.reshape(D, 3 * D), preferred_element_type=jnp.float32).astype(jnp.bfloat16)
    projected = lax.map(project, features.reshape(N_SEQ * N_SUB, HALF_TOK, D)).reshape(TOKENS, 3, HEADS, HDIM)
    queries = projected[:, 0]
    padding = jnp.zeros((CH, HEADS, HDIM), jnp.bfloat16)
    key_padded = jnp.concatenate([padding, projected[:, 1], padding], axis=0)
    value_padded = jnp.concatenate([padding, projected[:, 2], padding], axis=0)
    utterance_ends = jnp.cumsum(utt_lengths).astype(jnp.int32)
    positions = (jnp.arange(TOKENS + 2 * CH) - CH).astype(jnp.int32)
    utterance_ids = lax.optimization_barrier(jnp.sum((utterance_ends[None, :] <= positions[:, None]).astype(jnp.int32), axis=1)).astype(jnp.int32)
    key_inside = (positions >= 0) & (positions < TOKENS)
    relative_index = (jnp.arange(CH)[:, None] - jnp.arange(3 * CH)[None, :] + 3 * CH - 1).astype(jnp.int32)
    position_bias = rel_bias[:, relative_index]

    def attend(block_index):
        start = (block_index * CH).astype(jnp.int32)
        query_block = lax.dynamic_slice_in_dim(queries, start, CH, 0).astype(jnp.float32)
        key_block = lax.dynamic_slice_in_dim(key_padded, start, 3 * CH, 0).astype(jnp.float32)
        value_block = lax.dynamic_slice_in_dim(value_padded, start, 3 * CH, 0).astype(jnp.float32)
        query_utt = lax.dynamic_slice_in_dim(utterance_ids, start + CH, CH, 0)
        key_utt = lax.dynamic_slice_in_dim(utterance_ids, start, 3 * CH, 0)
        key_valid = lax.dynamic_slice_in_dim(key_inside, start, 3 * CH, 0)
        scores = jnp.einsum('qhd,khd->hqk', query_block, key_block) * (1.0 / math.sqrt(HDIM)) + position_bias
        allowed = (query_utt[:, None] == key_utt[None, :]) & key_valid[None, :]
        scores = jnp.where(allowed[None, :, :], scores, MASKED)
        row_peak = lax.optimization_barrier(jnp.max(scores, axis=2, keepdims=True))
        weights = jnp.exp(scores - row_peak)
        attention_weights = (weights / lax.optimization_barrier(jnp.sum(weights, axis=2, keepdims=True))).astype(jnp.bfloat16)
        context = jnp.einsum('hqk,khd->qhd', attention_weights.astype(jnp.float32), value_block)
        return context.astype(jnp.bfloat16).reshape(CH, D)
    contexts = lax.map(attend, jnp.arange(TOKENS // CH).astype(jnp.int32))
    return contexts.reshape(TOKENS, D)
```

```python
import functools
import math

import jax
import jax.numpy as jnp
import numpy as np
from jax import lax
from jax.experimental import pallas as pl
from jax.experimental.pallas import tpu as pltpu
from jax.sharding import PartitionSpec as P

HDIM = 64
MEL = 128
NFFT = 512
HOP = 160
FP = 17
CH = 136
PE = 32
LANES = 128
TABLE = 640


SAMPLE_RATE = 16000.0
EPSILON = 1e-05
MASKED = -1e30
MESH = pl.DeviceIdType.MESH


def split_bf16(table):
    high = table.astype(np.float32).astype(jnp.bfloat16)
    low = (table - high.astype(np.float64)).astype(np.float32).astype(jnp.bfloat16)
    return np.stack([high, low])


def window_table():
    return (0.5 - 0.5 * np.cos(2.0 * np.pi / NFFT * np.arange(NFFT)))[None].astype(np.float32)


def fourier_tables():
    half = NFFT // 2
    sample = np.arange(half)[:, None]

    def phase(bins):
        return (sample * bins[None, :] % NFFT) * (2.0 * np.pi / NFFT)

    even, odd = np.arange(0, half, 2), np.arange(1, half, 2)
    even_sine = np.sin(phase(even))
    even_sine[:, 0] = np.cos(phase(np.array([half])))[:, 0]
    even_table = np.concatenate([np.cos(phase(even)), even_sine], axis=1)
    odd_table = np.concatenate([np.cos(phase(odd)), np.sin(phase(odd))], axis=1)
    return np.stack([split_bf16(even_table), split_bf16(odd_table)])


def mel_table():
    bin_total = NFFT // 2 + 1
    highest = 2595.0 * math.log10(1.0 + SAMPLE_RATE / 2.0 / 700.0)
    points = np.arange(MEL + 2) * (highest / (MEL + 1))
    hertz = 700.0 * (np.power(10.0, points / 2595.0) - 1.0)
    centres = np.arange(bin_total) * (SAMPLE_RATE / NFFT)
    rising = (centres[:, None] - hertz[None, :-2]) / (hertz[1:-1] - hertz[:-2])[None, :]
    falling = (hertz[None, 2:] - centres[:, None]) / (hertz[2:] - hertz[1:-1])[None, :]
    table = np.maximum(0.0, np.minimum(rising, falling))
    sine_even = table[0 : bin_total - 1 : 2].copy()
    sine_even[0] = table[bin_total - 1]
    rows = np.concatenate(
        [table[0 : bin_total - 1 : 2], sine_even, table[1::2], table[1::2]], axis=0
    )
    return split_bf16(rows)


def dot(left, right):
    return jnp.dot(left, right, preferred_element_type=jnp.float32)


def dot_split(value, high, low):
    value_high = value.astype(jnp.bfloat16)
    value_low = (value - value_high.astype(jnp.float32)).astype(jnp.bfloat16)
    return dot(value_high, high) + dot(value_low, high) + dot(value_high, low)


def front_kernel(
    shards, heads, subs,
    wave_ref, target_ref, weight_ref, window_ref, fourier_ref, mel_ref,
    tokens_ref, weights_ref,
    mel_rows, packed, received,
    wsend, wrecv, fsend, frecv, asend, arecv, hsend, hrecv, nsend, nrecv,
):
    s, h, u = lax.axis_index("seq"), lax.axis_index("head"), lax.axis_index("sub")
    half = s * subs + u
    halves = shards * subs
    slots = wave_ref.shape[0]
    cap = slots // shards
    depth = weight_ref.shape[0] // subs

    def place_of(index):
        return {"seq": index // subs, "sub": index % subs}

    barrier = pltpu.get_barrier_semaphore()
    for d in range(1, shards):
        pl.semaphore_signal(
            barrier, inc=1, device_id={"seq": lax.rem(s + d, shards)}, device_id_type=MESH
        )
    for d in range(1, heads):
        pl.semaphore_signal(
            barrier, inc=1, device_id={"head": lax.rem(h + d, heads)}, device_id_type=MESH
        )

    @pl.when(half > 0)
    def _():
        for other in range(heads):
            pl.semaphore_signal(
                barrier, inc=1, device_id={**place_of(half - 1), "head": other},
                device_id_type=MESH,
            )

    @pl.when(half < halves - 1)
    def _():
        for other in range(heads):
            pl.semaphore_signal(
                barrier, inc=1, device_id={**place_of(half + 1), "head": other},
                device_id_type=MESH,
            )

    inner = jnp.where(half > 0, heads, 0) + jnp.where(half < halves - 1, heads, 0)
    pl.semaphore_wait(barrier, shards - 1 + heads - 1 + inner)

    weight_copies = []
    for d in range(1, heads):
        copy = pltpu.make_async_remote_copy(
            src_ref=weight_ref.at[pl.ds(u * depth, depth)],
            dst_ref=weights_ref.at[h, pl.ds(u * depth, depth)],
            send_sem=wsend.at[d - 1],
            recv_sem=wrecv.at[d - 1],
            device_id={"head": lax.rem(h + d, heads)},
            device_id_type=MESH,
        )
        copy.start()
        weight_copies.append(copy)

    for shift in range(4):
        wave = wave_ref[...]
        if shift:
            wave = pltpu.roll(wave, wave.shape[1] - 32 * shift, 1)
        groups = range((FP - shift + 3) // 4)
        frames = [
            wave[:, LANES * (5 * g + shift) : LANES * (5 * g + shift) + NFFT] * window_ref[...]
            for g in groups
        ]
        frames = jnp.concatenate(frames, axis=0)
        low, high = frames[:, : NFFT // 2], frames[:, NFFT // 2 :]
        even = dot_split(low + high, fourier_ref[0, 0], fourier_ref[0, 1])
        odd = dot_split(low - high, fourier_ref[1, 0], fourier_ref[1, 1])
        squares = jnp.concatenate([even * even, odd * odd], axis=1)
        energy = dot_split(squares, mel_ref[0], mel_ref[1])
        logs = jnp.log(1.0 + energy).astype(jnp.bfloat16)
        for g in groups:
            f = 4 * g + shift
            mel_rows[:, f * MEL : (f + 1) * MEL] = logs[g * slots : (g + 1) * slots]

    target = target_ref[...]
    owner = jnp.where(target >= 0, lax.shift_right_arithmetic(target, 5), shards)
    place = jnp.bitwise_and(target, PE - 1)
    down = lax.broadcasted_iota(jnp.int32, (slots, slots), 0)
    across = lax.broadcasted_iota(jnp.int32, (slots, slots), 1)
    owner_wide = jnp.broadcast_to(owner, (slots, slots))
    owner_down = jnp.sum(jnp.where(down == across, owner_wide, 0), axis=1, keepdims=True)
    rank = jnp.sum(
        jnp.where((owner_down == owner_wide) & (down < across), 1, 0), axis=0, keepdims=True
    )
    goal = jnp.where(owner < shards, owner * cap + rank, -1)
    chosen = down == goal
    select = chosen.astype(jnp.float32).astype(jnp.bfloat16)
    rows = dot(select, mel_rows[...]).astype(jnp.bfloat16)
    code = jnp.sum(jnp.where(chosen, place + 1, 0), axis=1, keepdims=True).astype(jnp.float32)
    code = jnp.broadcast_to(code, (slots, LANES)).astype(jnp.bfloat16)
    for t in range(shards):
        packed[t, :, : FP * MEL] = rows[t * cap : (t + 1) * cap]
        packed[t, :, FP * MEL :] = code[t * cap : (t + 1) * cap]

    piece_copies = []
    for d in range(1, shards):
        to = lax.rem(s + d, shards)
        copy = pltpu.make_async_remote_copy(
            src_ref=packed.at[to],
            dst_ref=received.at[s],
            send_sem=asend.at[d - 1],
            recv_sem=arecv.at[d - 1],
            device_id={"seq": to},
            device_id_type=MESH,
        )
        copy.start()
        piece_copies.append(copy)
    received[s] = packed[s]
    weights_ref[h] = weight_ref[...]

    @pl.when(half == 0)
    def _():
        tokens_ref[0] = jnp.zeros(tokens_ref.shape[1:], tokens_ref.dtype)

    @pl.when(half == halves - 1)
    def _():
        tokens_ref[heads + 1] = jnp.zeros(tokens_ref.shape[1:], tokens_ref.dtype)

    for copy in piece_copies:
        copy.wait_recv()

    arrived = received[...]
    if cap % 16:
        arrived = arrived.astype(jnp.float32).reshape(slots, arrived.shape[2])
        arrived = arrived.astype(jnp.bfloat16)
    else:
        arrived = arrived.reshape(slots, arrived.shape[2])
    frame_rows = jnp.concatenate(
        [arrived[:, f * MEL : (f + 1) * MEL] for f in range(FP)], axis=0
    )
    code_down = arrived[:, FP * MEL : FP * MEL + 1].astype(jnp.float32)
    code_wide = jnp.broadcast_to(code_down, (slots, slots))
    code_across = jnp.sum(jnp.where(down == across, code_wide, 0.0), axis=0, keepdims=True)
    first = jnp.where(code_across > 0.5, (code_across - 1.0) * FP, -1000.0)
    frame_at = jnp.concatenate([first + float(f) for f in range(FP)], axis=1)
    for m in range(4):
        token = lax.broadcasted_iota(jnp.int32, (CH, FP * slots), 0) * 4 + m
        pick = (token.astype(jnp.float32) == frame_at).astype(jnp.float32).astype(jnp.bfloat16)
        tokens_ref[h + 1, :, m * MEL : (m + 1) * MEL] = dot(pick, frame_rows).astype(jnp.bfloat16)

    head_copies = []
    for d in range(1, heads):
        copy = pltpu.make_async_remote_copy(
            src_ref=tokens_ref.at[h + 1],
            dst_ref=tokens_ref.at[h + 1],
            send_sem=hsend.at[d - 1],
            recv_sem=hrecv.at[d - 1],
            device_id={"head": lax.rem(h + d, heads)},
            device_id_type=MESH,
        )
        copy.start()
        head_copies.append(copy)

    def halo(other, to, row, side):
        return pltpu.make_async_remote_copy(
            src_ref=tokens_ref.at[h + 1],
            dst_ref=tokens_ref.at[row],
            send_sem=nsend.at[side, other],
            recv_sem=nrecv.at[side],
            device_id={**place_of(to), "head": other},
            device_id_type=MESH,
        )

    sends_up = (half < halves - 1) & (h == heads - 1)
    sends_down = (half > 0) & (h == 0)

    @pl.when(sends_up)
    def _():
        for other in range(heads):
            halo(other, half + 1, 0, 0).start()

    @pl.when(sends_down)
    def _():
        for other in range(heads):
            halo(other, half - 1, heads + 1, 1).start()

    sibling = {"sub": lax.rem(u + 1, subs)}
    forward_copies = []
    for d in range(1, heads):
        weight_copies[d - 1].wait_recv()
        source = lax.rem(h - d + heads, heads)
        copy = pltpu.make_async_remote_copy(
            src_ref=weights_ref.at[source, pl.ds(u * depth, depth)],
            dst_ref=weights_ref.at[source, pl.ds(u * depth, depth)],
            send_sem=fsend.at[d - 1],
            recv_sem=frecv.at[d - 1],
            device_id=sibling,
            device_id_type=MESH,
        )
        copy.start()
        forward_copies.append(copy)

    for copy in head_copies:
        copy.wait_recv()

    @pl.when(half > 0)
    def _():
        halo(0, half, 0, 0).wait_recv()

    @pl.when(half < halves - 1)
    def _():
        halo(0, half, heads + 1, 1).wait_recv()

    for copy in forward_copies:
        copy.wait_recv()
    for copy in weight_copies + piece_copies + head_copies + forward_copies:
        copy.wait_send()

    @pl.when(sends_up)
    def _():
        for other in range(heads):
            halo(other, half + 1, 0, 0).wait_send()

    @pl.when(sends_down)
    def _():
        for other in range(heads):
            halo(other, half - 1, heads + 1, 1).wait_send()


def back_kernel(
    tokens_ref, weights_ref, sub_bias_ref, gain_ref, qkv_ref, table_ref, lengths_ref, first_ref,
    context_ref,
    qkv_weight, queries, keys, values, bias, sem,
):
    blocks = tokens_ref.shape[0] - 2
    heads = weights_ref.shape[0]
    width = weights_ref.shape[2]
    loads = [
        pltpu.make_async_copy(qkv_ref.at[part], qkv_weight.at[part], sem.at[part])
        for part in range(3)
    ]
    for load in loads:
        load.start()
    first_token, token_total = first_ref[0], first_ref[1]

    normed = []
    for b in range(blocks + 2):
        summed = jnp.concatenate(
            [dot(tokens_ref[b], weights_ref[g]) for g in range(heads)], axis=1
        )
        summed = summed + sub_bias_ref[...].astype(jnp.float32)
        value = (summed / (1.0 + jnp.exp(-summed))).astype(jnp.bfloat16).astype(jnp.float32)
        mean = jnp.mean(value, axis=1, keepdims=True)
        centred = value - mean
        variance = jnp.mean(centred * centred, axis=1, keepdims=True)
        normed.append(
            (centred * lax.rsqrt(variance + EPSILON) * gain_ref[...]).astype(jnp.bfloat16)
        )

    for part, out in ((0, queries), (1, keys), (2, values)):
        loads[part].wait()
        for b in range(blocks + 2):
            if part == 0 and (b == 0 or b == blocks + 1):
                continue
            row = (b - 1 if part == 0 else b) * CH
            done = dot(normed[b], qkv_weight[part]).astype(jnp.bfloat16).astype(jnp.float32)
            if part == 0:
                done = done * (1.0 / math.sqrt(HDIM))
            out[row : row + CH] = done

    span = 3 * CH
    masks = []
    for b in range(blocks):
        query_pos = first_token + b * CH + lax.broadcasted_iota(jnp.int32, (CH, 1), 0)
        key_pos = first_token + (b - 1) * CH + lax.broadcasted_iota(jnp.int32, (1, span), 1)
        end = jnp.int32(0)
        query_utt = jnp.zeros_like(query_pos)
        key_utt = jnp.zeros_like(key_pos)
        for r in range(lengths_ref.shape[0]):
            end = end + lengths_ref[r]
            query_utt = query_utt + (query_pos >= end).astype(jnp.int32)
            key_utt = key_utt + (key_pos >= end).astype(jnp.int32)
        inside = (key_pos >= 0) & (key_pos < token_total)
        key_utt = jnp.where(inside, key_utt, -1)
        masks.append(query_utt == key_utt)

    lane = lax.broadcasted_iota(jnp.int32, (1, LANES), 1)
    for pair in range(width // LANES):
        lanes = slice(pair * LANES, (pair + 1) * LANES)
        for e in range(2):
            row = jnp.broadcast_to(table_ref[2 * pair + e : 2 * pair + e + 1, :], (CH, TABLE))
            rolled = pltpu.roll(row, TABLE - (CH - 1), 1, stride=1, stride_axis=0)
            bias[e] = rolled[:, :span]
        for b in range(blocks):
            query = queries[b * CH : (b + 1) * CH, lanes]
            key = keys[b * CH : b * CH + span, lanes].astype(jnp.bfloat16)
            value = values[b * CH : b * CH + span, lanes].astype(jnp.bfloat16)
            outs = []
            for e in range(2):
                mine = (lane < HDIM) if e == 0 else (lane >= HDIM)
                own = jnp.where(mine, query, 0.0).astype(jnp.bfloat16)
                scores = lax.dot_general(
                    own, key, (((1,), (1,)), ((), ())), preferred_element_type=jnp.float32
                )
                scores = jnp.where(masks[b], scores + bias[e], MASKED)
                raised = jnp.exp(scores - jnp.max(scores, axis=1, keepdims=True))
                share = 1.0 / jnp.sum(raised, axis=1, keepdims=True)
                outs.append(dot((raised * share).astype(jnp.bfloat16), value))
            joined = jnp.where(lane < HDIM, outs[0], outs[1]).astype(jnp.bfloat16)
            context_ref[b * CH : (b + 1) * CH, lanes] = joined


def local(
    shards, heads, subs,
    wave_pieces, piece_target, utt_lengths, sub_weight, sub_bias, norm_gain, qkv_weight, rel_bias,
):
    slots, samples = wave_pieces.shape[3:]
    cap = slots // shards
    depth, width = sub_weight.shape
    whole_width = qkv_weight.shape[0]
    vmem = pl.BlockSpec(memory_space=pltpu.VMEM)
    smem = pl.BlockSpec(memory_space=pltpu.SMEM)
    payload = (FP + 1) * MEL
    dma = pltpu.SemaphoreType.DMA
    tokens, weights = pl.pallas_call(
        functools.partial(front_kernel, shards, heads, subs),
        out_shape=(
            jax.ShapeDtypeStruct((heads + 2, CH, 4 * MEL), jnp.bfloat16),
            jax.ShapeDtypeStruct((heads, depth, width), jnp.bfloat16),
        ),
        in_specs=[vmem] * 6,
        out_specs=(vmem, vmem),
        scratch_shapes=[
            pltpu.VMEM((slots, FP * MEL), jnp.bfloat16),
            pltpu.VMEM((shards, cap, payload), jnp.bfloat16),
            pltpu.VMEM((shards, cap, payload), jnp.bfloat16),
            dma((heads - 1,)), dma((heads - 1,)), dma((heads - 1,)), dma((heads - 1,)),
            dma((shards - 1,)), dma((shards - 1,)),
            dma((heads - 1,)), dma((heads - 1,)),
            dma((2, heads)), dma((2,)),
        ],
        compiler_params=pltpu.CompilerParams(
            collective_id=0, has_side_effects=True, vmem_limit_bytes=48 << 20
        ),
        name="front",
    )(
        wave_pieces.reshape(slots, samples),
        piece_target.reshape(1, slots),
        sub_weight,
        jnp.asarray(window_table()),
        jnp.asarray(fourier_tables()),
        jnp.asarray(mel_table()),
    )

    tokens_here = heads * CH
    half = lax.axis_index("seq") * subs + lax.axis_index("sub")
    first = jnp.stack([half * tokens_here, jnp.int32(shards * subs * tokens_here)])
    bias_all = lax.all_gather(sub_bias, "head", axis=0, tiled=True)
    table = jnp.pad(rel_bias[:, ::-1], ((0, 0), (0, TABLE - rel_bias.shape[1])))
    return pl.pallas_call(
        back_kernel,
        out_shape=jax.ShapeDtypeStruct((tokens_here, width), jnp.bfloat16),
        in_specs=[vmem, vmem, vmem, vmem, pl.BlockSpec(memory_space=pl.ANY), vmem, smem, smem],
        out_specs=vmem,
        scratch_shapes=[
            pltpu.VMEM((3, whole_width, width), jnp.bfloat16),
            pltpu.VMEM((tokens_here, width), jnp.float32),
            pltpu.VMEM((tokens_here + 2 * CH, width), jnp.float32),
            pltpu.VMEM((tokens_here + 2 * CH, width), jnp.float32),
            pltpu.VMEM((2, CH, 3 * CH), jnp.float32),
            dma((3,)),
        ],
        compiler_params=pltpu.CompilerParams(vmem_limit_bytes=48 << 20),
        name="back",
    )(
        tokens,
        weights,
        bias_all.reshape(1, whole_width),
        norm_gain.reshape(1, whole_width),
        jnp.transpose(qkv_weight, (1, 0, 2)),
        table,
        utt_lengths,
        first,
    )


def solution(mesh):
    placed = (
        P(("groups", "seq"), "head", "sub", None, None),
        P(("groups", "seq"), "head", "sub", None),
        P("groups"),
        P(None, "head"),
        P("head"),
        P(),
        P(None, None, "head"),
        P("head", None),
    )
    return jax.shard_map(
        functools.partial(local, mesh.shape["seq"], mesh.shape["head"], mesh.shape["sub"]),
        mesh=mesh,
        in_specs=placed,
        out_specs=P(("groups", "seq", "sub"), "head"),
        check_vma=False,
    )
```

```python
import functools
import math

import jax
import jax.numpy as jnp
import numpy as np
from jax import lax
from jax.experimental import pallas as pl
from jax.experimental.pallas import tpu as pltpu
from jax.sharding import PartitionSpec as P

HDIM = 64
MEL = 128
NFFT = 512
HOP = 160
FP = 17
CH = 136
PE = 32
LANES = 128
TABLE = 640


SAMPLE_RATE = 16000.0
EPSILON = 1e-05
MASKED = -1e30
MESH = pl.DeviceIdType.MESH


def split_bf16(table):
    high = table.astype(np.float32).astype(jnp.bfloat16)
    low = (table - high.astype(np.float64)).astype(np.float32).astype(jnp.bfloat16)
    return np.stack([high, low])


def window_table():
    return (0.5 - 0.5 * np.cos(2.0 * np.pi / NFFT * np.arange(NFFT)))[None].astype(np.float32)


def fourier_tables():
    half = NFFT // 2
    sample = np.arange(half)[:, None]

    def phase(bins):
        return (sample * bins[None, :] % NFFT) * (2.0 * np.pi / NFFT)

    even, odd = np.arange(0, half, 2), np.arange(1, half, 2)
    even_sine = np.sin(phase(even))
    even_sine[:, 0] = np.cos(phase(np.array([half])))[:, 0]
    even_table = np.concatenate([np.cos(phase(even)), even_sine], axis=1)
    odd_table = np.concatenate([np.cos(phase(odd)), np.sin(phase(odd))], axis=1)
    return np.stack([split_bf16(even_table), split_bf16(odd_table)])


def mel_table():
    bin_total = NFFT // 2 + 1
    highest = 2595.0 * math.log10(1.0 + SAMPLE_RATE / 2.0 / 700.0)
    points = np.arange(MEL + 2) * (highest / (MEL + 1))
    hertz = 700.0 * (np.power(10.0, points / 2595.0) - 1.0)
    centres = np.arange(bin_total) * (SAMPLE_RATE / NFFT)
    rising = (centres[:, None] - hertz[None, :-2]) / (hertz[1:-1] - hertz[:-2])[None, :]
    falling = (hertz[None, 2:] - centres[:, None]) / (hertz[2:] - hertz[1:-1])[None, :]
    table = np.maximum(0.0, np.minimum(rising, falling))
    sine_even = table[0 : bin_total - 1 : 2].copy()
    sine_even[0] = table[bin_total - 1]
    rows = np.concatenate(
        [table[0 : bin_total - 1 : 2], sine_even, table[1::2], table[1::2]], axis=0
    )
    return split_bf16(rows)


def dot(left, right):
    return jnp.dot(left, right, preferred_element_type=jnp.float32)


def dot_split(value, high, low):
    value_high = value.astype(jnp.bfloat16)
    value_low = (value - value_high.astype(jnp.float32)).astype(jnp.bfloat16)
    return dot(value_high, high) + dot(value_low, high) + dot(value_high, low)


def front_kernel(
    shards, heads, subs,
    wave_in, target_in, weight_ref, window_in, fourier_in, mel_in, sub_bias_in, gain_in, rel_in,
    tokens_ref, weights_ref, sub_bias_ref, gain_ref, bias_ref,
    wave_ref, target_ref, window_ref, fourier_ref, mel_ref, sub_bias_row, gain_row, rel_ref,
    mel_rows, packed, received,
    lsem, wsend, wrecv, fsend, frecv, asend, arecv, hsend, hrecv, nsend, nrecv, bsend, brecv,
):
    s, h, u = lax.axis_index("seq"), lax.axis_index("head"), lax.axis_index("sub")
    half = s * subs + u
    halves = shards * subs
    slots = wave_ref.shape[0]
    cap = slots // shards
    depth = weight_ref.shape[0] // subs

    def place_of(index):
        return {"seq": index // subs, "sub": index % subs}

    pairs = (
        (wave_in, wave_ref), (window_in, window_ref), (fourier_in, fourier_ref),
        (mel_in, mel_ref), (target_in, target_ref), (sub_bias_in, sub_bias_row),
        (gain_in, gain_row), (rel_in, rel_ref), (weight_ref, weights_ref.at[h]),
    )
    loads = [pltpu.make_async_copy(a, b, lsem.at[i]) for i, (a, b) in enumerate(pairs)]
    for load in loads:
        load.start()

    barrier = pltpu.get_barrier_semaphore()
    for d in range(1, shards):
        pl.semaphore_signal(
            barrier, inc=1, device_id={"seq": lax.rem(s + d, shards)}, device_id_type=MESH
        )
    for d in range(1, heads):
        pl.semaphore_signal(
            barrier, inc=1, device_id={"head": lax.rem(h + d, heads)}, device_id_type=MESH
        )

    @pl.when(half > 0)
    def _():
        for other in range(heads):
            pl.semaphore_signal(
                barrier, inc=1, device_id={**place_of(half - 1), "head": other},
                device_id_type=MESH,
            )

    @pl.when(half < halves - 1)
    def _():
        for other in range(heads):
            pl.semaphore_signal(
                barrier, inc=1, device_id={**place_of(half + 1), "head": other},
                device_id_type=MESH,
            )

    inner = jnp.where(half > 0, heads, 0) + jnp.where(half < halves - 1, heads, 0)
    pl.semaphore_wait(barrier, shards - 1 + heads - 1 + inner)

    weight_copies, bias_copies = [], []
    for d in range(1, heads):
        copy = pltpu.make_async_remote_copy(
            src_ref=weight_ref.at[pl.ds(u * depth, depth)],
            dst_ref=weights_ref.at[h, pl.ds(u * depth, depth)],
            send_sem=wsend.at[d - 1],
            recv_sem=wrecv.at[d - 1],
            device_id={"head": lax.rem(h + d, heads)},
            device_id_type=MESH,
        )
        copy.start()
        weight_copies.append(copy)

    loads[5].wait()
    sub_bias_ref[h] = sub_bias_row[...].astype(jnp.float32).reshape(1, sub_bias_row.shape[0])
    for d in range(1, heads):
        copy = pltpu.make_async_remote_copy(
            src_ref=sub_bias_ref.at[h],
            dst_ref=sub_bias_ref.at[h],
            send_sem=bsend.at[d - 1],
            recv_sem=brecv.at[d - 1],
            device_id={"head": lax.rem(h + d, heads)},
            device_id_type=MESH,
        )
        copy.start()
        bias_copies.append(copy)

    for index in range(4):
        loads[index].wait()
    for shift in range(4):
        wave = wave_ref[...]
        if shift:
            wave = pltpu.roll(wave, wave.shape[1] - 32 * shift, 1)
        groups = range((FP - shift + 3) // 4)
        frames = [
            wave[:, LANES * (5 * g + shift) : LANES * (5 * g + shift) + NFFT] * window_ref[...]
            for g in groups
        ]
        frames = jnp.concatenate(frames, axis=0)
        low, high = frames[:, : NFFT // 2], frames[:, NFFT // 2 :]
        even = dot_split(low + high, fourier_ref[0, 0], fourier_ref[0, 1])
        odd = dot_split(low - high, fourier_ref[1, 0], fourier_ref[1, 1])
        squares = jnp.concatenate([even * even, odd * odd], axis=1)
        energy = dot_split(squares, mel_ref[0], mel_ref[1])
        logs = jnp.log(1.0 + energy).astype(jnp.bfloat16)
        for g in groups:
            f = 4 * g + shift
            mel_rows[:, f * MEL : (f + 1) * MEL] = logs[g * slots : (g + 1) * slots]

    loads[4].wait()
    target = target_ref[...]
    owner = jnp.where(target >= 0, lax.shift_right_arithmetic(target, 5), shards)
    place = jnp.bitwise_and(target, PE - 1)
    down = lax.broadcasted_iota(jnp.int32, (slots, slots), 0)
    across = lax.broadcasted_iota(jnp.int32, (slots, slots), 1)
    owner_wide = jnp.broadcast_to(owner, (slots, slots))
    owner_down = jnp.sum(jnp.where(down == across, owner_wide, 0), axis=1, keepdims=True)
    rank = jnp.sum(
        jnp.where((owner_down == owner_wide) & (down < across), 1, 0), axis=0, keepdims=True
    )
    goal = jnp.where(owner < shards, owner * cap + rank, -1)
    chosen = down == goal
    select = chosen.astype(jnp.float32).astype(jnp.bfloat16)
    rows = dot(select, mel_rows[...]).astype(jnp.bfloat16)
    code = jnp.sum(jnp.where(chosen, place + 1, 0), axis=1, keepdims=True).astype(jnp.float32)
    code = jnp.broadcast_to(code, (slots, LANES)).astype(jnp.bfloat16)
    for t in range(shards):
        packed[t, :, : FP * MEL] = rows[t * cap : (t + 1) * cap]
        packed[t, :, FP * MEL :] = code[t * cap : (t + 1) * cap]

    piece_copies = []
    for d in range(1, shards):
        to = lax.rem(s + d, shards)
        copy = pltpu.make_async_remote_copy(
            src_ref=packed.at[to],
            dst_ref=received.at[s],
            send_sem=asend.at[d - 1],
            recv_sem=arecv.at[d - 1],
            device_id={"seq": to},
            device_id_type=MESH,
        )
        copy.start()
        piece_copies.append(copy)
    received[s] = packed[s]

    @pl.when(half == 0)
    def _():
        tokens_ref[0] = jnp.zeros(tokens_ref.shape[1:], tokens_ref.dtype)

    @pl.when(half == halves - 1)
    def _():
        tokens_ref[heads + 1] = jnp.zeros(tokens_ref.shape[1:], tokens_ref.dtype)

    loads[6].wait()
    gain_ref[...] = gain_row[...].reshape(gain_ref.shape)
    loads[7].wait()
    taps = rel_ref.shape[1]
    mirror = lax.broadcasted_iota(jnp.int32, (taps, TABLE), 0) + lax.broadcasted_iota(
        jnp.int32, (taps, TABLE), 1
    )
    mirror = (mirror == taps - 1).astype(jnp.float32).astype(jnp.bfloat16)
    rest = rel_ref[...]
    terms = []
    for _ in range(3):
        term = rest.astype(jnp.bfloat16)
        rest = rest - term.astype(jnp.float32)
        terms.append(dot(term, mirror))
    flipped = terms[0] + (terms[1] + terms[2])
    for row in range(rel_ref.shape[0]):
        wide = jnp.broadcast_to(flipped[row : row + 1, :], (CH, TABLE))
        rolled = pltpu.roll(wide, TABLE - (CH - 1), 1, stride=1, stride_axis=0)
        bias_ref[row] = rolled[:, : 3 * CH]

    for copy in piece_copies:
        copy.wait_recv()

    arrived = received[...]
    if cap % 16:
        arrived = arrived.astype(jnp.float32).reshape(slots, arrived.shape[2])
        arrived = arrived.astype(jnp.bfloat16)
    else:
        arrived = arrived.reshape(slots, arrived.shape[2])
    frame_rows = jnp.concatenate(
        [arrived[:, f * MEL : (f + 1) * MEL] for f in range(FP)], axis=0
    )
    code_down = arrived[:, FP * MEL : FP * MEL + 1].astype(jnp.float32)
    code_wide = jnp.broadcast_to(code_down, (slots, slots))
    code_across = jnp.sum(jnp.where(down == across, code_wide, 0.0), axis=0, keepdims=True)
    first = jnp.where(code_across > 0.5, (code_across - 1.0) * FP, -1000.0)
    frame_at = jnp.concatenate([first + float(f) for f in range(FP)], axis=1)
    for m in range(4):
        token = lax.broadcasted_iota(jnp.int32, (CH, FP * slots), 0) * 4 + m
        pick = (token.astype(jnp.float32) == frame_at).astype(jnp.float32).astype(jnp.bfloat16)
        tokens_ref[h + 1, :, m * MEL : (m + 1) * MEL] = dot(pick, frame_rows).astype(jnp.bfloat16)

    head_copies = []
    for d in range(1, heads):
        copy = pltpu.make_async_remote_copy(
            src_ref=tokens_ref.at[h + 1],
            dst_ref=tokens_ref.at[h + 1],
            send_sem=hsend.at[d - 1],
            recv_sem=hrecv.at[d - 1],
            device_id={"head": lax.rem(h + d, heads)},
            device_id_type=MESH,
        )
        copy.start()
        head_copies.append(copy)

    def halo(other, to, row, side):
        return pltpu.make_async_remote_copy(
            src_ref=tokens_ref.at[h + 1],
            dst_ref=tokens_ref.at[row],
            send_sem=nsend.at[side, other],
            recv_sem=nrecv.at[side],
            device_id={**place_of(to), "head": other},
            device_id_type=MESH,
        )

    sends_up = (half < halves - 1) & (h == heads - 1)
    sends_down = (half > 0) & (h == 0)

    @pl.when(sends_up)
    def _():
        for other in range(heads):
            halo(other, half + 1, 0, 0).start()

    @pl.when(sends_down)
    def _():
        for other in range(heads):
            halo(other, half - 1, heads + 1, 1).start()

    sibling = {"sub": lax.rem(u + 1, subs)}
    forward_copies = []
    for d in range(1, heads):
        weight_copies[d - 1].wait_recv()
        source = lax.rem(h - d + heads, heads)
        copy = pltpu.make_async_remote_copy(
            src_ref=weights_ref.at[source, pl.ds(u * depth, depth)],
            dst_ref=weights_ref.at[source, pl.ds(u * depth, depth)],
            send_sem=fsend.at[d - 1],
            recv_sem=frecv.at[d - 1],
            device_id=sibling,
            device_id_type=MESH,
        )
        copy.start()
        forward_copies.append(copy)

    for copy in head_copies:
        copy.wait_recv()

    @pl.when(half > 0)
    def _():
        halo(0, half, 0, 0).wait_recv()

    @pl.when(half < halves - 1)
    def _():
        halo(0, half, heads + 1, 1).wait_recv()

    for copy in forward_copies + bias_copies:
        copy.wait_recv()
    loads[8].wait()
    for copy in bias_copies + weight_copies + piece_copies + head_copies + forward_copies:
        copy.wait_send()

    @pl.when(sends_up)
    def _():
        for other in range(heads):
            halo(other, half + 1, 0, 0).wait_send()

    @pl.when(sends_down)
    def _():
        for other in range(heads):
            halo(other, half - 1, heads + 1, 1).wait_send()


def back_kernel(
    shards, subs,
    tokens_ref, weights_ref, sub_bias_ref, gain_ref, bias_ref, qkv_ref, lengths_in,
    context_ref,
    qkv_weight, queries, keys, values, lengths_ref, sem,
):
    blocks = tokens_ref.shape[0] - 2
    heads = weights_ref.shape[0]
    width = weights_ref.shape[2]
    loads = [
        pltpu.make_async_copy(qkv_ref.at[part], qkv_weight.at[part], sem.at[part])
        for part in range(3)
    ]
    loads.append(pltpu.make_async_copy(lengths_in, lengths_ref, sem.at[3]))
    for load in loads:
        load.start()
    half = lax.axis_index("seq") * subs + lax.axis_index("sub")
    first_token, token_total = half * blocks * CH, shards * subs * blocks * CH

    normed = []
    for b in range(blocks + 2):
        summed = jnp.concatenate(
            [dot(tokens_ref[b], weights_ref[g]) + sub_bias_ref[g] for g in range(heads)], axis=1
        )
        value = (summed / (1.0 + jnp.exp(-summed))).astype(jnp.bfloat16).astype(jnp.float32)
        mean = jnp.mean(value, axis=1, keepdims=True)
        centred = value - mean
        variance = jnp.mean(centred * centred, axis=1, keepdims=True)
        normed.append(
            (centred * lax.rsqrt(variance + EPSILON) * gain_ref[...]).astype(jnp.bfloat16)
        )

    for part, out in ((0, queries), (1, keys), (2, values)):
        loads[part].wait()
        for b in range(blocks + 2):
            if part == 0 and (b == 0 or b == blocks + 1):
                continue
            row = (b - 1 if part == 0 else b) * CH
            done = dot(normed[b], qkv_weight[part]).astype(jnp.bfloat16).astype(jnp.float32)
            if part == 0:
                done = done * (1.0 / math.sqrt(HDIM))
            out[row : row + CH] = done

    loads[3].wait()
    span = 3 * CH
    masks = []
    for b in range(blocks):
        query_pos = first_token + b * CH + lax.broadcasted_iota(jnp.int32, (CH, 1), 0)
        key_pos = first_token + (b - 1) * CH + lax.broadcasted_iota(jnp.int32, (1, span), 1)
        end = jnp.int32(0)
        query_utt = jnp.zeros_like(query_pos)
        key_utt = jnp.zeros_like(key_pos)
        for r in range(lengths_ref.shape[0]):
            end = end + lengths_ref[r]
            query_utt = query_utt + (query_pos >= end).astype(jnp.int32)
            key_utt = key_utt + (key_pos >= end).astype(jnp.int32)
        inside = (key_pos >= 0) & (key_pos < token_total)
        key_utt = jnp.where(inside, key_utt, -1)
        masks.append(query_utt == key_utt)

    lane = lax.broadcasted_iota(jnp.int32, (1, LANES), 1)
    for pair in range(width // LANES):
        lanes = slice(pair * LANES, (pair + 1) * LANES)
        for b in range(blocks):
            query = queries[b * CH : (b + 1) * CH, lanes]
            key = keys[b * CH : b * CH + span, lanes].astype(jnp.bfloat16)
            value = values[b * CH : b * CH + span, lanes].astype(jnp.bfloat16)
            outs = []
            for e in range(2):
                mine = (lane < HDIM) if e == 0 else (lane >= HDIM)
                own = jnp.where(mine, query, 0.0).astype(jnp.bfloat16)
                scores = lax.dot_general(
                    own, key, (((1,), (1,)), ((), ())), preferred_element_type=jnp.float32
                )
                scores = jnp.where(masks[b], scores + bias_ref[2 * pair + e], MASKED)
                raised = jnp.exp(scores - jnp.max(scores, axis=1, keepdims=True))
                share = 1.0 / jnp.sum(raised, axis=1, keepdims=True)
                outs.append(dot((raised * share).astype(jnp.bfloat16), value))
            joined = jnp.where(lane < HDIM, outs[0], outs[1]).astype(jnp.bfloat16)
            context_ref[b * CH : (b + 1) * CH, lanes] = joined


def local(
    shards, heads, subs,
    wave_pieces, piece_target, utt_lengths, sub_weight, sub_bias, norm_gain, qkv_weight, rel_bias,
):
    slots, samples = wave_pieces.shape[3:]
    cap = slots // shards
    depth, width = sub_weight.shape
    whole_width = qkv_weight.shape[0]
    vmem = pl.BlockSpec(memory_space=pltpu.VMEM)
    payload = (FP + 1) * MEL
    dma = pltpu.SemaphoreType.DMA
    hbm = pl.BlockSpec(memory_space=pltpu.HBM)
    heads_here = rel_bias.shape[0]
    tokens, weights, bias_rows, gain_row, position_bias = pl.pallas_call(
        functools.partial(front_kernel, shards, heads, subs),
        out_shape=(
            jax.ShapeDtypeStruct((heads + 2, CH, 4 * MEL), jnp.bfloat16),
            jax.ShapeDtypeStruct((heads, depth, width), jnp.bfloat16),
            jax.ShapeDtypeStruct((heads, 1, width), jnp.float32),
            jax.ShapeDtypeStruct((1, whole_width), jnp.float32),
            jax.ShapeDtypeStruct((heads_here, CH, 3 * CH), jnp.float32),
        ),
        in_specs=[hbm] * 9,
        out_specs=(vmem,) * 5,
        scratch_shapes=[
            pltpu.VMEM((slots, samples), jnp.float32),
            pltpu.VMEM((1, slots), jnp.int32),
            pltpu.VMEM((1, NFFT), jnp.float32),
            pltpu.VMEM((2, 2, NFFT // 2, NFFT // 2), jnp.bfloat16),
            pltpu.VMEM((2, NFFT, MEL), jnp.bfloat16),
            pltpu.VMEM((width,), jnp.bfloat16),
            pltpu.VMEM((whole_width,), jnp.float32),
            pltpu.VMEM(rel_bias.shape, jnp.float32),
            pltpu.VMEM((slots, FP * MEL), jnp.bfloat16),
            pltpu.VMEM((shards, cap, payload), jnp.bfloat16),
            pltpu.VMEM((shards, cap, payload), jnp.bfloat16),
            dma((9,)),
            dma((heads - 1,)), dma((heads - 1,)), dma((heads - 1,)), dma((heads - 1,)),
            dma((shards - 1,)), dma((shards - 1,)),
            dma((heads - 1,)), dma((heads - 1,)),
            dma((2, heads)), dma((2,)), dma((heads - 1,)), dma((heads - 1,)),
        ],
        compiler_params=pltpu.CompilerParams(
            collective_id=0, has_side_effects=True, vmem_limit_bytes=28 << 20
        ),
        name="front",
    )(
        *[
            pltpu.with_memory_space_constraint(value, pltpu.HBM)
            for value in (
                wave_pieces.reshape(slots, samples),
                piece_target.reshape(1, slots),
                sub_weight,
                jnp.asarray(window_table()),
                jnp.asarray(fourier_tables()),
                jnp.asarray(mel_table()),
                sub_bias,
                norm_gain,
                rel_bias,
            )
        ]
    )

    tokens_here = heads * CH
    return pl.pallas_call(
        functools.partial(back_kernel, shards, subs),
        out_shape=jax.ShapeDtypeStruct((tokens_here, width), jnp.bfloat16),
        in_specs=[vmem] * 5 + [hbm, hbm],
        out_specs=vmem,
        scratch_shapes=[
            pltpu.VMEM((3, whole_width, width), jnp.bfloat16),
            pltpu.VMEM((tokens_here, width), jnp.float32),
            pltpu.VMEM((tokens_here + 2 * CH, width), jnp.float32),
            pltpu.VMEM((tokens_here + 2 * CH, width), jnp.float32),
            pltpu.SMEM(utt_lengths.shape, jnp.int32),
            dma((4,)),
        ],
        compiler_params=pltpu.CompilerParams(vmem_limit_bytes=36 << 20),
        name="back",
    )(
        tokens,
        weights,
        bias_rows,
        gain_row,
        position_bias,
        pltpu.with_memory_space_constraint(jnp.transpose(qkv_weight, (1, 0, 2)), pltpu.HBM),
        pltpu.with_memory_space_constraint(utt_lengths, pltpu.HBM),
    )


def solution(mesh):
    placed = (
        P(("groups", "seq"), "head", "sub", None, None),
        P(("groups", "seq"), "head", "sub", None),
        P("groups"),
        P(None, "head"),
        P("head"),
        P(),
        P(None, None, "head"),
        P("head", None),
    )
    return jax.shard_map(
        functools.partial(local, mesh.shape["seq"], mesh.shape["head"], mesh.shape["sub"]),
        mesh=mesh,
        in_specs=placed,
        out_specs=P(("groups", "seq", "sub"), "head"),
        check_vma=False,
    )
```

```python
import functools
import math

import jax
import jax.numpy as jnp
import numpy as np
from jax import lax
from jax.experimental import pallas as pl
from jax.experimental.pallas import tpu as pltpu
from jax.sharding import PartitionSpec as P

HDIM = 64
MEL = 128
NFFT = 512
HOP = 160
FP = 17
CH = 136
PE = 32
LANES = 128
TABLE = 640


SAMPLE_RATE = 16000.0
EPSILON = 1e-05
MASKED = -1e30
MESH = pl.DeviceIdType.MESH


def split_bf16(table):
    high = table.astype(np.float32).astype(jnp.bfloat16)
    low = (table - high.astype(np.float64)).astype(np.float32).astype(jnp.bfloat16)
    return np.stack([high, low])


def window_table():
    return (0.5 - 0.5 * np.cos(2.0 * np.pi / NFFT * np.arange(NFFT)))[None].astype(np.float32)


def fourier_tables():
    half = NFFT // 2
    sample = np.arange(half)[:, None]

    def phase(bins):
        return (sample * bins[None, :] % NFFT) * (2.0 * np.pi / NFFT)

    even, odd = np.arange(0, half, 2), np.arange(1, half, 2)
    even_sine = np.sin(phase(even))
    even_sine[:, 0] = np.cos(phase(np.array([half])))[:, 0]
    even_table = np.concatenate([np.cos(phase(even)), even_sine], axis=1)
    odd_table = np.concatenate([np.cos(phase(odd)), np.sin(phase(odd))], axis=1)
    return np.stack([split_bf16(even_table), split_bf16(odd_table)])


def mel_table():
    bin_total = NFFT // 2 + 1
    highest = 2595.0 * math.log10(1.0 + SAMPLE_RATE / 2.0 / 700.0)
    points = np.arange(MEL + 2) * (highest / (MEL + 1))
    hertz = 700.0 * (np.power(10.0, points / 2595.0) - 1.0)
    centres = np.arange(bin_total) * (SAMPLE_RATE / NFFT)
    rising = (centres[:, None] - hertz[None, :-2]) / (hertz[1:-1] - hertz[:-2])[None, :]
    falling = (hertz[None, 2:] - centres[:, None]) / (hertz[2:] - hertz[1:-1])[None, :]
    table = np.maximum(0.0, np.minimum(rising, falling))
    sine_even = table[0 : bin_total - 1 : 2].copy()
    sine_even[0] = table[bin_total - 1]
    rows = np.concatenate(
        [table[0 : bin_total - 1 : 2], sine_even, table[1::2], table[1::2]], axis=0
    )
    return split_bf16(rows)


def dot(left, right):
    return jnp.dot(left, right, preferred_element_type=jnp.float32)


def dot_split(value, high, low):
    value_high = value.astype(jnp.bfloat16)
    value_low = (value - value_high.astype(jnp.float32)).astype(jnp.bfloat16)
    return dot(value_high, high) + dot(value_low, high) + dot(value_high, low)


def front_kernel(
    shards, heads, subs,
    wave_in, target_in, weight_ref, window_in, fourier_in, mel_in, sub_bias_in, gain_in, rel_in,
    tokens_ref, weights_ref, sub_bias_ref, gain_ref, bias_ref,
    wave_ref, target_ref, window_ref, fourier_ref, mel_ref, sub_bias_row, gain_row, rel_ref,
    packed_0, packed_1, packed_2, packed_3, received_0, received_1, received_2, received_3,
    lsem, wsend, wrecv, fsend, frecv, asend, arecv, hsend, hrecv, nsend, nrecv, bsend, brecv,
):
    s, h, u = lax.axis_index("seq"), lax.axis_index("head"), lax.axis_index("sub")
    half = s * subs + u
    halves = shards * subs
    slots = wave_ref.shape[0]
    cap = slots // shards
    depth = weight_ref.shape[0] // subs

    packed = (packed_0, packed_1, packed_2, packed_3)
    received = (received_0, received_1, received_2, received_3)

    def place_of(index):
        return {"seq": index // subs, "sub": index % subs}

    pairs = (
        (wave_in, wave_ref), (window_in, window_ref), (fourier_in, fourier_ref),
        (mel_in, mel_ref), (target_in, target_ref), (sub_bias_in, sub_bias_row),
        (gain_in, gain_row), (rel_in, rel_ref), (weight_ref, weights_ref.at[h]),
    )
    loads = [pltpu.make_async_copy(a, b, lsem.at[i]) for i, (a, b) in enumerate(pairs)]
    for load in loads:
        load.start()

    barrier = pltpu.get_barrier_semaphore()
    for d in range(1, shards):
        pl.semaphore_signal(
            barrier, inc=1, device_id={"seq": lax.rem(s + d, shards)}, device_id_type=MESH
        )
    for d in range(1, heads):
        pl.semaphore_signal(
            barrier, inc=1, device_id={"head": lax.rem(h + d, heads)}, device_id_type=MESH
        )

    @pl.when(half > 0)
    def _():
        for other in range(heads):
            pl.semaphore_signal(
                barrier, inc=1, device_id={**place_of(half - 1), "head": other},
                device_id_type=MESH,
            )

    @pl.when(half < halves - 1)
    def _():
        for other in range(heads):
            pl.semaphore_signal(
                barrier, inc=1, device_id={**place_of(half + 1), "head": other},
                device_id_type=MESH,
            )

    inner = jnp.where(half > 0, heads, 0) + jnp.where(half < halves - 1, heads, 0)
    pl.semaphore_wait(barrier, shards - 1 + heads - 1 + inner)

    weight_copies, bias_copies = [], []
    for d in range(1, heads):
        copy = pltpu.make_async_remote_copy(
            src_ref=weight_ref.at[pl.ds(u * depth, depth)],
            dst_ref=weights_ref.at[h, pl.ds(u * depth, depth)],
            send_sem=wsend.at[d - 1],
            recv_sem=wrecv.at[d - 1],
            device_id={"head": lax.rem(h + d, heads)},
            device_id_type=MESH,
        )
        copy.start()
        weight_copies.append(copy)

    loads[5].wait()
    sub_bias_ref[h] = sub_bias_row[...].astype(jnp.float32).reshape(1, sub_bias_row.shape[0])
    for d in range(1, heads):
        copy = pltpu.make_async_remote_copy(
            src_ref=sub_bias_ref.at[h],
            dst_ref=sub_bias_ref.at[h],
            send_sem=bsend.at[d - 1],
            recv_sem=brecv.at[d - 1],
            device_id={"head": lax.rem(h + d, heads)},
            device_id_type=MESH,
        )
        copy.start()
        bias_copies.append(copy)

    loads[4].wait()
    target = target_ref[...]
    owner = jnp.where(target >= 0, lax.shift_right_arithmetic(target, 5), shards)
    place = jnp.bitwise_and(target, PE - 1)
    down = lax.broadcasted_iota(jnp.int32, (slots, slots), 0)
    across = lax.broadcasted_iota(jnp.int32, (slots, slots), 1)
    owner_wide = jnp.broadcast_to(owner, (slots, slots))
    owner_down = jnp.sum(jnp.where(down == across, owner_wide, 0), axis=1, keepdims=True)
    rank = jnp.sum(
        jnp.where((owner_down == owner_wide) & (down < across), 1, 0), axis=0, keepdims=True
    )
    goal = jnp.where(owner < shards, owner * cap + rank, -1)
    chosen = down == goal
    select = chosen.astype(jnp.float32).astype(jnp.bfloat16)
    code = jnp.sum(jnp.where(chosen, place + 1, 0), axis=1, keepdims=True).astype(jnp.float32)
    code = jnp.broadcast_to(code, (slots, LANES)).astype(jnp.bfloat16)

    piece_copies = []
    for index in range(4):
        loads[index].wait()
    for shift in range(4):
        wave = wave_ref[...]
        if shift:
            wave = pltpu.roll(wave, wave.shape[1] - 32 * shift, 1)
        groups = range((FP - shift + 3) // 4)
        frames = [
            wave[:, LANES * (5 * g + shift) : LANES * (5 * g + shift) + NFFT] * window_ref[...]
            for g in groups
        ]
        frames = jnp.concatenate(frames, axis=0)
        low, high = frames[:, : NFFT // 2], frames[:, NFFT // 2 :]
        even = dot_split(low + high, fourier_ref[0, 0], fourier_ref[0, 1])
        odd = dot_split(low - high, fourier_ref[1, 0], fourier_ref[1, 1])
        squares = jnp.concatenate([even * even, odd * odd], axis=1)
        energy = dot_split(squares, mel_ref[0], mel_ref[1])
        logs = jnp.log(1.0 + energy).astype(jnp.bfloat16)
        logs = jnp.concatenate([logs[g * slots : (g + 1) * slots] for g in groups], axis=1)
        rows = dot(select, logs).astype(jnp.bfloat16)
        wide = len(groups) * MEL
        for t in range(shards):
            packed[shift][t, :, :wide] = rows[t * cap : (t + 1) * cap]
            if shift == 0:
                packed[0][t, :, wide:] = code[t * cap : (t + 1) * cap]
        for d in range(1, shards):
            to = lax.rem(s + d, shards)
            copy = pltpu.make_async_remote_copy(
                src_ref=packed[shift].at[to],
                dst_ref=received[shift].at[s],
                send_sem=asend.at[shift, d - 1],
                recv_sem=arecv.at[shift, d - 1],
                device_id={"seq": to},
                device_id_type=MESH,
            )
            copy.start()
            piece_copies.append(copy)
        received[shift][s] = packed[shift][s]

    @pl.when(half == 0)
    def _():
        tokens_ref[0] = jnp.zeros(tokens_ref.shape[1:], tokens_ref.dtype)

    @pl.when(half == halves - 1)
    def _():
        tokens_ref[heads + 1] = jnp.zeros(tokens_ref.shape[1:], tokens_ref.dtype)

    loads[6].wait()
    gain_ref[...] = gain_row[...].reshape(gain_ref.shape)
    loads[7].wait()
    taps = rel_ref.shape[1]
    mirror = lax.broadcasted_iota(jnp.int32, (taps, TABLE), 0) + lax.broadcasted_iota(
        jnp.int32, (taps, TABLE), 1
    )
    mirror = (mirror == taps - 1).astype(jnp.float32).astype(jnp.bfloat16)
    rest = rel_ref[...]
    terms = []
    for _ in range(3):
        term = rest.astype(jnp.bfloat16)
        rest = rest - term.astype(jnp.float32)
        terms.append(dot(term, mirror))
    flipped = terms[0] + (terms[1] + terms[2])
    for row in range(rel_ref.shape[0]):
        wide = jnp.broadcast_to(flipped[row : row + 1, :], (CH, TABLE))
        rolled = pltpu.roll(wide, TABLE - (CH - 1), 1, stride=1, stride_axis=0)
        bias_ref[row] = rolled[:, : 3 * CH]

    totals = [jnp.zeros((CH, MEL), jnp.float32) for _ in range(4)]
    for shift in range(4):
        for d in range(1, shards):
            piece_copies[shift * (shards - 1) + d - 1].wait_recv()
        arrived = received[shift][...]
        if cap % 16:
            arrived = arrived.astype(jnp.float32).reshape(slots, arrived.shape[2])
            arrived = arrived.astype(jnp.bfloat16)
        else:
            arrived = arrived.reshape(slots, arrived.shape[2])
        groups = range((FP - shift + 3) // 4)
        frame_rows = jnp.concatenate(
            [arrived[:, g * MEL : (g + 1) * MEL] for g in groups], axis=0
        )
        if shift == 0:
            code_down = arrived[:, len(groups) * MEL : len(groups) * MEL + 1].astype(jnp.float32)
            code_wide = jnp.broadcast_to(code_down, (slots, slots))
            code_across = jnp.sum(
                jnp.where(down == across, code_wide, 0.0), axis=0, keepdims=True
            )
            first = jnp.where(code_across > 0.5, (code_across - 1.0) * FP, -1000.0)
        frame_at = jnp.concatenate([first + float(4 * g + shift) for g in groups], axis=1)
        for m in range(4):
            token = lax.broadcasted_iota(jnp.int32, (CH, len(groups) * slots), 0) * 4 + m
            pick = (token.astype(jnp.float32) == frame_at).astype(jnp.float32)
            totals[m] = totals[m] + dot(pick.astype(jnp.bfloat16), frame_rows)
    for m in range(4):
        tokens_ref[h + 1, :, m * MEL : (m + 1) * MEL] = totals[m].astype(jnp.bfloat16)

    head_copies = []
    for d in range(1, heads):
        copy = pltpu.make_async_remote_copy(
            src_ref=tokens_ref.at[h + 1],
            dst_ref=tokens_ref.at[h + 1],
            send_sem=hsend.at[d - 1],
            recv_sem=hrecv.at[d - 1],
            device_id={"head": lax.rem(h + d, heads)},
            device_id_type=MESH,
        )
        copy.start()
        head_copies.append(copy)

    def halo(other, to, row, side):
        return pltpu.make_async_remote_copy(
            src_ref=tokens_ref.at[h + 1],
            dst_ref=tokens_ref.at[row],
            send_sem=nsend.at[side, other],
            recv_sem=nrecv.at[side],
            device_id={**place_of(to), "head": other},
            device_id_type=MESH,
        )

    sends_up = (half < halves - 1) & (h == heads - 1)
    sends_down = (half > 0) & (h == 0)

    @pl.when(sends_up)
    def _():
        for other in range(heads):
            halo(other, half + 1, 0, 0).start()

    @pl.when(sends_down)
    def _():
        for other in range(heads):
            halo(other, half - 1, heads + 1, 1).start()

    sibling = {"sub": lax.rem(u + 1, subs)}
    forward_copies = []
    for d in range(1, heads):
        weight_copies[d - 1].wait_recv()
        source = lax.rem(h - d + heads, heads)
        copy = pltpu.make_async_remote_copy(
            src_ref=weights_ref.at[source, pl.ds(u * depth, depth)],
            dst_ref=weights_ref.at[source, pl.ds(u * depth, depth)],
            send_sem=fsend.at[d - 1],
            recv_sem=frecv.at[d - 1],
            device_id=sibling,
            device_id_type=MESH,
        )
        copy.start()
        forward_copies.append(copy)

    for copy in head_copies:
        copy.wait_recv()

    @pl.when(half > 0)
    def _():
        halo(0, half, 0, 0).wait_recv()

    @pl.when(half < halves - 1)
    def _():
        halo(0, half, heads + 1, 1).wait_recv()

    for copy in forward_copies + bias_copies:
        copy.wait_recv()
    loads[8].wait()
    for copy in bias_copies + weight_copies + piece_copies + head_copies + forward_copies:
        copy.wait_send()

    @pl.when(sends_up)
    def _():
        for other in range(heads):
            halo(other, half + 1, 0, 0).wait_send()

    @pl.when(sends_down)
    def _():
        for other in range(heads):
            halo(other, half - 1, heads + 1, 1).wait_send()


def back_kernel(
    shards, subs,
    tokens_ref, weights_ref, sub_bias_ref, gain_ref, bias_ref, qkv_ref, lengths_in,
    context_ref,
    qkv_weight, queries, keys, values, lengths_ref, sem,
):
    blocks = tokens_ref.shape[0] // CH - 2
    heads = weights_ref.shape[0]
    width = weights_ref.shape[2]
    loads = [
        pltpu.make_async_copy(qkv_ref.at[part], qkv_weight.at[part], sem.at[part])
        for part in range(3)
    ]
    loads.append(pltpu.make_async_copy(lengths_in, lengths_ref, sem.at[3]))
    for load in loads:
        load.start()
    half = lax.axis_index("seq") * subs + lax.axis_index("sub")
    first_token, token_total = half * blocks * CH, shards * subs * blocks * CH

    tokens = tokens_ref[...]
    summed = jnp.concatenate(
        [dot(tokens, weights_ref[g]) + sub_bias_ref[g] for g in range(heads)], axis=1
    )
    value = (summed / (1.0 + jnp.exp(-summed))).astype(jnp.bfloat16).astype(jnp.float32)
    mean = jnp.mean(value, axis=1, keepdims=True)
    centred = value - mean
    variance = jnp.mean(centred * centred, axis=1, keepdims=True)
    normed = centred * lax.rsqrt(variance + EPSILON) * gain_ref[...]
    normed_all = normed.astype(jnp.bfloat16)
    normed_own = normed[CH : (blocks + 1) * CH].astype(jnp.bfloat16)

    for part, out in ((0, queries), (1, keys), (2, values)):
        loads[part].wait()
        rows = normed_own if part == 0 else normed_all
        done = dot(rows, qkv_weight[part]).astype(jnp.bfloat16).astype(jnp.float32)
        out[...] = done * (1.0 / math.sqrt(HDIM)) if part == 0 else done

    loads[3].wait()
    span = 3 * CH
    masks = []
    for b in range(blocks):
        query_pos = first_token + b * CH + lax.broadcasted_iota(jnp.int32, (CH, 1), 0)
        key_pos = first_token + (b - 1) * CH + lax.broadcasted_iota(jnp.int32, (1, span), 1)
        end = jnp.int32(0)
        query_utt = jnp.zeros_like(query_pos)
        key_utt = jnp.zeros_like(key_pos)
        for r in range(lengths_ref.shape[0]):
            end = end + lengths_ref[r]
            query_utt = query_utt + (query_pos >= end).astype(jnp.int32)
            key_utt = key_utt + (key_pos >= end).astype(jnp.int32)
        inside = (key_pos >= 0) & (key_pos < token_total)
        key_utt = jnp.where(inside, key_utt, -1)
        mask = jnp.where(query_utt == key_utt, 1.0, 0.0)
        masks.append(jnp.concatenate([mask, mask], axis=0) > 0.5)

    lane = lax.broadcasted_iota(jnp.int32, (1, LANES), 1)
    for pair in range(width // LANES):
        lanes = slice(pair * LANES, (pair + 1) * LANES)
        shift = bias_ref[2 * pair : 2 * pair + 2].reshape(2 * CH, span)
        for b in range(blocks):
            query = queries[b * CH : (b + 1) * CH, lanes]
            key = keys[b * CH : b * CH + span, lanes].astype(jnp.bfloat16)
            value = values[b * CH : b * CH + span, lanes].astype(jnp.bfloat16)
            both = jnp.concatenate(
                [jnp.where(lane < HDIM, query, 0.0), jnp.where(lane < HDIM, 0.0, query)], axis=0
            ).astype(jnp.bfloat16)
            scores = lax.dot_general(
                both, key, (((1,), (1,)), ((), ())), preferred_element_type=jnp.float32
            )
            scores = jnp.where(masks[b], scores + shift, MASKED)
            raised = jnp.exp(scores - jnp.max(scores, axis=1, keepdims=True))
            share = 1.0 / jnp.sum(raised, axis=1, keepdims=True)
            out = dot((raised * share).astype(jnp.bfloat16), value)
            joined = jnp.where(lane < HDIM, out[:CH], out[CH:]).astype(jnp.bfloat16)
            context_ref[b * CH : (b + 1) * CH, lanes] = joined


def local(
    shards, heads, subs,
    wave_pieces, piece_target, utt_lengths, sub_weight, sub_bias, norm_gain, qkv_weight, rel_bias,
):
    slots, samples = wave_pieces.shape[3:]
    cap = slots // shards
    depth, width = sub_weight.shape
    whole_width = qkv_weight.shape[0]
    vmem = pl.BlockSpec(memory_space=pltpu.VMEM)
    payloads = [((FP - shift + 3) // 4 + (shift == 0)) * MEL for shift in range(4)]
    dma = pltpu.SemaphoreType.DMA
    hbm = pl.BlockSpec(memory_space=pltpu.HBM)
    heads_here = rel_bias.shape[0]
    tokens, weights, bias_rows, gain_row, position_bias = pl.pallas_call(
        functools.partial(front_kernel, shards, heads, subs),
        out_shape=(
            jax.ShapeDtypeStruct((heads + 2, CH, 4 * MEL), jnp.bfloat16),
            jax.ShapeDtypeStruct((heads, depth, width), jnp.bfloat16),
            jax.ShapeDtypeStruct((heads, 1, width), jnp.float32),
            jax.ShapeDtypeStruct((1, whole_width), jnp.float32),
            jax.ShapeDtypeStruct((heads_here, CH, 3 * CH), jnp.float32),
        ),
        in_specs=[hbm] * 9,
        out_specs=(vmem,) * 5,
        scratch_shapes=[
            pltpu.VMEM((slots, samples), jnp.float32),
            pltpu.VMEM((1, slots), jnp.int32),
            pltpu.VMEM((1, NFFT), jnp.float32),
            pltpu.VMEM((2, 2, NFFT // 2, NFFT // 2), jnp.bfloat16),
            pltpu.VMEM((2, NFFT, MEL), jnp.bfloat16),
            pltpu.VMEM((width,), jnp.bfloat16),
            pltpu.VMEM((whole_width,), jnp.float32),
            pltpu.VMEM(rel_bias.shape, jnp.float32),
            *[pltpu.VMEM((shards, cap, wide), jnp.bfloat16) for wide in payloads],
            *[pltpu.VMEM((shards, cap, wide), jnp.bfloat16) for wide in payloads],
            dma((9,)),
            dma((heads - 1,)), dma((heads - 1,)), dma((heads - 1,)), dma((heads - 1,)),
            dma((4, shards - 1)), dma((4, shards - 1)),
            dma((heads - 1,)), dma((heads - 1,)),
            dma((2, heads)), dma((2,)), dma((heads - 1,)), dma((heads - 1,)),
        ],
        compiler_params=pltpu.CompilerParams(
            collective_id=0, has_side_effects=True, vmem_limit_bytes=28 << 20
        ),
        name="front",
    )(
        *[
            pltpu.with_memory_space_constraint(value, pltpu.HBM)
            for value in (
                wave_pieces.reshape(slots, samples),
                piece_target.reshape(1, slots),
                sub_weight,
                jnp.asarray(window_table()),
                jnp.asarray(fourier_tables()),
                jnp.asarray(mel_table()),
                sub_bias,
                norm_gain,
                rel_bias,
            )
        ]
    )

    tokens_here = heads * CH
    return pl.pallas_call(
        functools.partial(back_kernel, shards, subs),
        out_shape=jax.ShapeDtypeStruct((tokens_here, width), jnp.bfloat16),
        in_specs=[vmem] * 5 + [hbm, hbm],
        out_specs=vmem,
        scratch_shapes=[
            pltpu.VMEM((3, whole_width, width), jnp.bfloat16),
            pltpu.VMEM((tokens_here, width), jnp.float32),
            pltpu.VMEM((tokens_here + 2 * CH, width), jnp.float32),
            pltpu.VMEM((tokens_here + 2 * CH, width), jnp.float32),
            pltpu.SMEM(utt_lengths.shape, jnp.int32),
            dma((4,)),
        ],
        compiler_params=pltpu.CompilerParams(vmem_limit_bytes=36 << 20),
        name="back",
    )(
        tokens.reshape((heads + 2) * CH, 4 * MEL),
        weights,
        bias_rows,
        gain_row,
        position_bias,
        pltpu.with_memory_space_constraint(jnp.transpose(qkv_weight, (1, 0, 2)), pltpu.HBM),
        pltpu.with_memory_space_constraint(utt_lengths, pltpu.HBM),
    )


def solution(mesh):
    placed = (
        P(("groups", "seq"), "head", "sub", None, None),
        P(("groups", "seq"), "head", "sub", None),
        P("groups"),
        P(None, "head"),
        P("head"),
        P(),
        P(None, None, "head"),
        P("head", None),
    )
    return jax.shard_map(
        functools.partial(local, mesh.shape["seq"], mesh.shape["head"], mesh.shape["sub"]),
        mesh=mesh,
        in_specs=placed,
        out_specs=P(("groups", "seq", "sub"), "head"),
        check_vma=False,
    )
```

```python
import functools
import math

import jax
import jax.numpy as jnp
import numpy as np
from jax import lax
from jax.experimental import pallas as pl
from jax.experimental.pallas import tpu as pltpu
from jax.sharding import PartitionSpec as P

HDIM = 64
MEL = 128
NFFT = 512
HOP = 160
FP = 17
CH = 136
PE = 32
LANES = 128
TABLE = 640


SAMPLE_RATE = 16000.0
EPSILON = 1e-05
MASKED = -1e30
MESH = pl.DeviceIdType.MESH


def split_bf16(table):
    high = table.astype(np.float32).astype(jnp.bfloat16)
    low = (table - high.astype(np.float64)).astype(np.float32).astype(jnp.bfloat16)
    return np.stack([high, low])


def window_table():
    return (0.5 - 0.5 * np.cos(2.0 * np.pi / NFFT * np.arange(NFFT)))[None].astype(np.float32)


def fourier_tables():
    half = NFFT // 2
    sample = np.arange(half)[:, None]

    def phase(bins):
        return (sample * bins[None, :] % NFFT) * (2.0 * np.pi / NFFT)

    even, odd = np.arange(0, half, 2), np.arange(1, half, 2)
    even_sine = np.sin(phase(even))
    even_sine[:, 0] = np.cos(phase(np.array([half])))[:, 0]
    even_table = np.concatenate([np.cos(phase(even)), even_sine], axis=1)
    odd_table = np.concatenate([np.cos(phase(odd)), np.sin(phase(odd))], axis=1)
    return np.stack([split_bf16(even_table), split_bf16(odd_table)])


def mel_table():
    bin_total = NFFT // 2 + 1
    highest = 2595.0 * math.log10(1.0 + SAMPLE_RATE / 2.0 / 700.0)
    points = np.arange(MEL + 2) * (highest / (MEL + 1))
    hertz = 700.0 * (np.power(10.0, points / 2595.0) - 1.0)
    centres = np.arange(bin_total) * (SAMPLE_RATE / NFFT)
    rising = (centres[:, None] - hertz[None, :-2]) / (hertz[1:-1] - hertz[:-2])[None, :]
    falling = (hertz[None, 2:] - centres[:, None]) / (hertz[2:] - hertz[1:-1])[None, :]
    table = np.maximum(0.0, np.minimum(rising, falling))
    sine_even = table[0 : bin_total - 1 : 2].copy()
    sine_even[0] = table[bin_total - 1]
    rows = np.concatenate(
        [table[0 : bin_total - 1 : 2], sine_even, table[1::2], table[1::2]], axis=0
    )
    return split_bf16(rows)


def dot(left, right):
    return jnp.dot(left, right, preferred_element_type=jnp.float32)


def dot_split(value, high, low):
    value_high = value.astype(jnp.bfloat16)
    value_low = (value - value_high.astype(jnp.float32)).astype(jnp.bfloat16)
    return dot(value_high, high) + dot(value_low, high) + dot(value_high, low)


def front_kernel(
    shards, heads, subs,
    wave_in, target_in, weight_ref, window_in, fourier_in, mel_in, sub_bias_in, gain_in, rel_in,
    tokens_ref, weights_ref, sub_bias_ref, gain_ref, bias_ref,
    wave_ref, target_ref, window_ref, fourier_ref, mel_ref, sub_bias_row, gain_row, rel_ref,
    packed_0, packed_1, packed_2, packed_3, received_0, received_1, received_2, received_3,
    lsem, wsend, wrecv, fsend, frecv, asend, arecv, hsend, hrecv, nsend, nrecv, bsend, brecv,
):
    s, h, u = lax.axis_index("seq"), lax.axis_index("head"), lax.axis_index("sub")
    half = s * subs + u
    halves = shards * subs
    slots = wave_ref.shape[0]
    cap = slots // shards
    depth = weight_ref.shape[0] // subs

    packed = (packed_0, packed_1, packed_2, packed_3)
    received = (received_0, received_1, received_2, received_3)

    def place_of(index):
        return {"seq": index // subs, "sub": index % subs}

    pairs = (
        (wave_in, wave_ref), (window_in, window_ref), (fourier_in, fourier_ref),
        (mel_in, mel_ref), (target_in, target_ref), (sub_bias_in, sub_bias_row),
        (gain_in, gain_row), (rel_in, rel_ref), (weight_ref, weights_ref.at[h]),
    )
    loads = [pltpu.make_async_copy(a, b, lsem.at[i]) for i, (a, b) in enumerate(pairs)]
    for load in loads:
        load.start()

    barrier = pltpu.get_barrier_semaphore()
    for d in range(1, shards):
        pl.semaphore_signal(
            barrier, inc=1, device_id={"seq": lax.rem(s + d, shards)}, device_id_type=MESH
        )
    for d in range(1, heads):
        pl.semaphore_signal(
            barrier, inc=1, device_id={"head": lax.rem(h + d, heads)}, device_id_type=MESH
        )

    @pl.when(half > 0)
    def _():
        pl.semaphore_signal(barrier, inc=1, device_id=place_of(half - 1), device_id_type=MESH)

    @pl.when(half < halves - 1)
    def _():
        pl.semaphore_signal(barrier, inc=1, device_id=place_of(half + 1), device_id_type=MESH)

    inner = jnp.where(half > 0, 1, 0) + jnp.where(half < halves - 1, 1, 0)
    pl.semaphore_wait(barrier, shards - 1 + heads - 1 + inner)

    weight_copies, bias_copies = [], []
    for d in range(1, heads):
        copy = pltpu.make_async_remote_copy(
            src_ref=weight_ref.at[pl.ds(u * depth, depth)],
            dst_ref=weights_ref.at[h, pl.ds(u * depth, depth)],
            send_sem=wsend.at[d - 1],
            recv_sem=wrecv.at[d - 1],
            device_id={"head": lax.rem(h + d, heads)},
            device_id_type=MESH,
        )
        copy.start()
        weight_copies.append(copy)

    loads[5].wait()
    sub_bias_ref[h] = sub_bias_row[...].astype(jnp.float32).reshape(1, sub_bias_row.shape[0])
    for d in range(1, heads):
        copy = pltpu.make_async_remote_copy(
            src_ref=sub_bias_ref.at[h],
            dst_ref=sub_bias_ref.at[h],
            send_sem=bsend.at[d - 1],
            recv_sem=brecv.at[d - 1],
            device_id={"head": lax.rem(h + d, heads)},
            device_id_type=MESH,
        )
        copy.start()
        bias_copies.append(copy)

    loads[4].wait()
    target = target_ref[...]
    owner = jnp.where(target >= 0, lax.shift_right_arithmetic(target, 5), shards)
    place = jnp.bitwise_and(target, PE - 1)
    down = lax.broadcasted_iota(jnp.int32, (slots, slots), 0)
    across = lax.broadcasted_iota(jnp.int32, (slots, slots), 1)
    owner_wide = jnp.broadcast_to(owner, (slots, slots))
    owner_down = jnp.sum(jnp.where(down == across, owner_wide, 0), axis=1, keepdims=True)
    rank = jnp.sum(
        jnp.where((owner_down == owner_wide) & (down < across), 1, 0), axis=0, keepdims=True
    )
    goal = jnp.where(owner < shards, owner * cap + rank, -1)
    chosen = down == goal
    select = chosen.astype(jnp.float32).astype(jnp.bfloat16)
    code = jnp.sum(jnp.where(chosen, place + 1, 0), axis=1, keepdims=True).astype(jnp.float32)
    code = jnp.broadcast_to(code, (slots, LANES)).astype(jnp.bfloat16)

    piece_copies = []
    for index in range(4):
        loads[index].wait()
    for shift in range(4):
        wave = wave_ref[...]
        if shift:
            wave = pltpu.roll(wave, wave.shape[1] - 32 * shift, 1)
        groups = range((FP - shift + 3) // 4)
        frames = [
            wave[:, LANES * (5 * g + shift) : LANES * (5 * g + shift) + NFFT] * window_ref[...]
            for g in groups
        ]
        frames = jnp.concatenate(frames, axis=0)
        low, high = frames[:, : NFFT // 2], frames[:, NFFT // 2 :]
        even = dot_split(low + high, fourier_ref[0, 0], fourier_ref[0, 1])
        odd = dot_split(low - high, fourier_ref[1, 0], fourier_ref[1, 1])
        squares = jnp.concatenate([even * even, odd * odd], axis=1)
        energy = dot_split(squares, mel_ref[0], mel_ref[1])
        logs = jnp.log(1.0 + energy).astype(jnp.bfloat16)
        logs = jnp.concatenate([logs[g * slots : (g + 1) * slots] for g in groups], axis=1)
        rows = dot(select, logs).astype(jnp.bfloat16)
        wide = len(groups) * MEL
        for t in range(shards):
            packed[shift][t, :, :wide] = rows[t * cap : (t + 1) * cap]
            if shift == 0:
                packed[0][t, :, wide:] = code[t * cap : (t + 1) * cap]
        for d in range(1, shards):
            to = lax.rem(s + d, shards)
            copy = pltpu.make_async_remote_copy(
                src_ref=packed[shift].at[to],
                dst_ref=received[shift].at[s],
                send_sem=asend.at[shift, d - 1],
                recv_sem=arecv.at[shift, d - 1],
                device_id={"seq": to},
                device_id_type=MESH,
            )
            copy.start()
            piece_copies.append(copy)
        received[shift][s] = packed[shift][s]

    @pl.when(half == 0)
    def _():
        tokens_ref[0] = jnp.zeros(tokens_ref.shape[1:], tokens_ref.dtype)

    @pl.when(half == halves - 1)
    def _():
        tokens_ref[heads + 1] = jnp.zeros(tokens_ref.shape[1:], tokens_ref.dtype)

    loads[6].wait()
    gain_ref[...] = gain_row[...].reshape(gain_ref.shape)
    loads[7].wait()
    taps = rel_ref.shape[1]
    mirror = lax.broadcasted_iota(jnp.int32, (taps, TABLE), 0) + lax.broadcasted_iota(
        jnp.int32, (taps, TABLE), 1
    )
    mirror = (mirror == taps - 1).astype(jnp.float32).astype(jnp.bfloat16)
    rest = rel_ref[...]
    terms = []
    for _ in range(3):
        term = rest.astype(jnp.bfloat16)
        rest = rest - term.astype(jnp.float32)
        terms.append(dot(term, mirror))
    flipped = terms[0] + (terms[1] + terms[2])
    for row in range(rel_ref.shape[0]):
        wide = jnp.broadcast_to(flipped[row : row + 1, :], (CH, TABLE))
        rolled = pltpu.roll(wide, TABLE - (CH - 1), 1, stride=1, stride_axis=0)
        bias_ref[row] = rolled[:, : 3 * CH]

    totals = [jnp.zeros((CH, MEL), jnp.float32) for _ in range(4)]
    for shift in range(4):
        for d in range(1, shards):
            piece_copies[shift * (shards - 1) + d - 1].wait_recv()
        arrived = received[shift][...]
        if cap % 16:
            arrived = arrived.astype(jnp.float32).reshape(slots, arrived.shape[2])
            arrived = arrived.astype(jnp.bfloat16)
        else:
            arrived = arrived.reshape(slots, arrived.shape[2])
        groups = range((FP - shift + 3) // 4)
        frame_rows = jnp.concatenate(
            [arrived[:, g * MEL : (g + 1) * MEL] for g in groups], axis=0
        )
        if shift == 0:
            code_down = arrived[:, len(groups) * MEL : len(groups) * MEL + 1].astype(jnp.float32)
            code_wide = jnp.broadcast_to(code_down, (slots, slots))
            code_across = jnp.sum(
                jnp.where(down == across, code_wide, 0.0), axis=0, keepdims=True
            )
            first = jnp.where(code_across > 0.5, (code_across - 1.0) * FP, -1000.0)
        frame_at = jnp.concatenate([first + float(4 * g + shift) for g in groups], axis=1)
        for m in range(4):
            token = lax.broadcasted_iota(jnp.int32, (CH, len(groups) * slots), 0) * 4 + m
            pick = (token.astype(jnp.float32) == frame_at).astype(jnp.float32)
            totals[m] = totals[m] + dot(pick.astype(jnp.bfloat16), frame_rows)
    for m in range(4):
        tokens_ref[h + 1, :, m * MEL : (m + 1) * MEL] = totals[m].astype(jnp.bfloat16)

    runs = ((0, 64), (64, CH - 64))
    head_copies = []
    for run, (start, size) in enumerate(runs):
        for d in range(1, heads):
            copy = pltpu.make_async_remote_copy(
                src_ref=tokens_ref.at[h + 1, pl.ds(start, size)],
                dst_ref=tokens_ref.at[h + 1, pl.ds(start, size)],
                send_sem=hsend.at[run, d - 1],
                recv_sem=hrecv.at[run, d - 1],
                device_id={"head": lax.rem(h + d, heads)},
                device_id_type=MESH,
            )
            copy.start()
            head_copies.append(copy)

    def halo(to, source, row, side, run):
        start, size = runs[run]
        return pltpu.make_async_remote_copy(
            src_ref=tokens_ref.at[source, pl.ds(start, size)],
            dst_ref=tokens_ref.at[row, pl.ds(start, size)],
            send_sem=nsend.at[side, run],
            recv_sem=nrecv.at[side, run],
            device_id=place_of(to),
            device_id_type=MESH,
        )

    def halo_up(run):
        return halo(half + 1, heads, 0, 0, run)

    def halo_down(run):
        return halo(half - 1, 1, heads + 1, 1, run)

    def when(condition, action):
        @pl.when(condition)
        def _():
            action()

    has_up, has_down = half < halves - 1, half > 0
    for run in range(2):
        when(has_up & (h == heads - 1), lambda: halo_up(run).start())
        when(has_down & (h == 0), lambda: halo_down(run).start())

    sibling = {"sub": lax.rem(u + 1, subs)}
    forward_copies = []
    for d in range(1, heads):
        weight_copies[d - 1].wait_recv()
        source = lax.rem(h - d + heads, heads)
        copy = pltpu.make_async_remote_copy(
            src_ref=weights_ref.at[source, pl.ds(u * depth, depth)],
            dst_ref=weights_ref.at[source, pl.ds(u * depth, depth)],
            send_sem=fsend.at[d - 1],
            recv_sem=frecv.at[d - 1],
            device_id=sibling,
            device_id_type=MESH,
        )
        copy.start()
        forward_copies.append(copy)

    for run in range(2):
        for d in range(1, heads):
            head_copies[run * (heads - 1) + d - 1].wait_recv()
        when(has_up & (h != heads - 1), lambda: halo_up(run).start())
        when(has_down & (h != 0), lambda: halo_down(run).start())

    for run in range(2):
        when(has_down, lambda: halo_up(run).wait_recv())
        when(has_up, lambda: halo_down(run).wait_recv())

    for copy in forward_copies + bias_copies:
        copy.wait_recv()
    loads[8].wait()
    for copy in bias_copies + weight_copies + piece_copies + head_copies + forward_copies:
        copy.wait_send()

    for run in range(2):
        when(has_up, lambda: halo_up(run).wait_send())
        when(has_down, lambda: halo_down(run).wait_send())


def back_kernel(
    shards, subs,
    tokens_ref, weights_ref, sub_bias_ref, gain_ref, bias_ref, qkv_ref, lengths_in,
    context_ref,
    qkv_weight, queries, keys, values, lengths_ref, sem,
):
    blocks = tokens_ref.shape[0] // CH - 2
    heads = weights_ref.shape[0]
    width = weights_ref.shape[2]
    loads = [
        pltpu.make_async_copy(qkv_ref.at[part], qkv_weight.at[part], sem.at[part])
        for part in range(3)
    ]
    loads.append(pltpu.make_async_copy(lengths_in, lengths_ref, sem.at[3]))
    for load in loads:
        load.start()
    half = lax.axis_index("seq") * subs + lax.axis_index("sub")
    first_token, token_total = half * blocks * CH, shards * subs * blocks * CH

    tokens = tokens_ref[...]
    summed = jnp.concatenate(
        [dot(tokens, weights_ref[g]) + sub_bias_ref[g] for g in range(heads)], axis=1
    )
    value = (summed / (1.0 + jnp.exp(-summed))).astype(jnp.bfloat16).astype(jnp.float32)
    mean = jnp.mean(value, axis=1, keepdims=True)
    centred = value - mean
    variance = jnp.mean(centred * centred, axis=1, keepdims=True)
    normed = centred * lax.rsqrt(variance + EPSILON) * gain_ref[...]
    normed_all = normed.astype(jnp.bfloat16)
    normed_own = normed[CH : (blocks + 1) * CH].astype(jnp.bfloat16)

    for part, out in ((0, queries), (1, keys), (2, values)):
        loads[part].wait()
        rows = normed_own if part == 0 else normed_all
        done = dot(rows, qkv_weight[part]).astype(jnp.bfloat16).astype(jnp.float32)
        out[...] = done * (1.0 / math.sqrt(HDIM)) if part == 0 else done

    loads[3].wait()
    span = 3 * CH
    masks = []
    for b in range(blocks):
        query_pos = first_token + b * CH + lax.broadcasted_iota(jnp.int32, (CH, 1), 0)
        key_pos = first_token + (b - 1) * CH + lax.broadcasted_iota(jnp.int32, (1, span), 1)
        end = jnp.int32(0)
        query_utt = jnp.zeros_like(query_pos)
        key_utt = jnp.zeros_like(key_pos)
        for r in range(lengths_ref.shape[0]):
            end = end + lengths_ref[r]
            query_utt = query_utt + (query_pos >= end).astype(jnp.int32)
            key_utt = key_utt + (key_pos >= end).astype(jnp.int32)
        inside = (key_pos >= 0) & (key_pos < token_total)
        key_utt = jnp.where(inside, key_utt, -1)
        mask = jnp.where(query_utt == key_utt, 1.0, 0.0)
        masks.append(jnp.concatenate([mask, mask], axis=0) > 0.5)

    lane = lax.broadcasted_iota(jnp.int32, (1, LANES), 1)
    for pair in range(width // LANES):
        lanes = slice(pair * LANES, (pair + 1) * LANES)
        shift = bias_ref[2 * pair : 2 * pair + 2].reshape(2 * CH, span)
        for b in range(blocks):
            query = queries[b * CH : (b + 1) * CH, lanes]
            key = keys[b * CH : b * CH + span, lanes].astype(jnp.bfloat16)
            value = values[b * CH : b * CH + span, lanes].astype(jnp.bfloat16)
            both = jnp.concatenate(
                [jnp.where(lane < HDIM, query, 0.0), jnp.where(lane < HDIM, 0.0, query)], axis=0
            ).astype(jnp.bfloat16)
            scores = lax.dot_general(
                both, key, (((1,), (1,)), ((), ())), preferred_element_type=jnp.float32
            )
            scores = jnp.where(masks[b], scores + shift, MASKED)
            raised = jnp.exp(scores - jnp.max(scores, axis=1, keepdims=True))
            share = 1.0 / jnp.sum(raised, axis=1, keepdims=True)
            out = dot((raised * share).astype(jnp.bfloat16), value)
            joined = jnp.where(lane < HDIM, out[:CH], out[CH:]).astype(jnp.bfloat16)
            context_ref[b * CH : (b + 1) * CH, lanes] = joined


def local(
    shards, heads, subs,
    wave_pieces, piece_target, utt_lengths, sub_weight, sub_bias, norm_gain, qkv_weight, rel_bias,
):
    slots, samples = wave_pieces.shape[3:]
    cap = slots // shards
    depth, width = sub_weight.shape
    whole_width = qkv_weight.shape[0]
    vmem = pl.BlockSpec(memory_space=pltpu.VMEM)
    payloads = [((FP - shift + 3) // 4 + (shift == 0)) * MEL for shift in range(4)]
    dma = pltpu.SemaphoreType.DMA
    hbm = pl.BlockSpec(memory_space=pltpu.HBM)
    heads_here = rel_bias.shape[0]
    tokens, weights, bias_rows, gain_row, position_bias = pl.pallas_call(
        functools.partial(front_kernel, shards, heads, subs),
        out_shape=(
            jax.ShapeDtypeStruct((heads + 2, CH, 4 * MEL), jnp.bfloat16),
            jax.ShapeDtypeStruct((heads, depth, width), jnp.bfloat16),
            jax.ShapeDtypeStruct((heads, 1, width), jnp.float32),
            jax.ShapeDtypeStruct((1, whole_width), jnp.float32),
            jax.ShapeDtypeStruct((heads_here, CH, 3 * CH), jnp.float32),
        ),
        in_specs=[hbm] * 9,
        out_specs=(vmem,) * 5,
        scratch_shapes=[
            pltpu.VMEM((slots, samples), jnp.float32),
            pltpu.VMEM((1, slots), jnp.int32),
            pltpu.VMEM((1, NFFT), jnp.float32),
            pltpu.VMEM((2, 2, NFFT // 2, NFFT // 2), jnp.bfloat16),
            pltpu.VMEM((2, NFFT, MEL), jnp.bfloat16),
            pltpu.VMEM((width,), jnp.bfloat16),
            pltpu.VMEM((whole_width,), jnp.float32),
            pltpu.VMEM(rel_bias.shape, jnp.float32),
            *[pltpu.VMEM((shards, cap, wide), jnp.bfloat16) for wide in payloads],
            *[pltpu.VMEM((shards, cap, wide), jnp.bfloat16) for wide in payloads],
            dma((9,)),
            dma((heads - 1,)), dma((heads - 1,)), dma((heads - 1,)), dma((heads - 1,)),
            dma((4, shards - 1)), dma((4, shards - 1)),
            dma((2, heads - 1)), dma((2, heads - 1)),
            dma((2, 2)), dma((2, 2)), dma((heads - 1,)), dma((heads - 1,)),
        ],
        compiler_params=pltpu.CompilerParams(
            collective_id=0, has_side_effects=True, vmem_limit_bytes=28 << 20
        ),
        name="front",
    )(
        *[
            pltpu.with_memory_space_constraint(value, pltpu.HBM)
            for value in (
                wave_pieces.reshape(slots, samples),
                piece_target.reshape(1, slots),
                sub_weight,
                jnp.asarray(window_table()),
                jnp.asarray(fourier_tables()),
                jnp.asarray(mel_table()),
                sub_bias,
                norm_gain,
                rel_bias,
            )
        ]
    )

    tokens_here = heads * CH
    return pl.pallas_call(
        functools.partial(back_kernel, shards, subs),
        out_shape=jax.ShapeDtypeStruct((tokens_here, width), jnp.bfloat16),
        in_specs=[vmem] * 5 + [hbm, hbm],
        out_specs=vmem,
        scratch_shapes=[
            pltpu.VMEM((3, whole_width, width), jnp.bfloat16),
            pltpu.VMEM((tokens_here, width), jnp.float32),
            pltpu.VMEM((tokens_here + 2 * CH, width), jnp.float32),
            pltpu.VMEM((tokens_here + 2 * CH, width), jnp.float32),
            pltpu.SMEM(utt_lengths.shape, jnp.int32),
            dma((4,)),
        ],
        compiler_params=pltpu.CompilerParams(vmem_limit_bytes=36 << 20),
        name="back",
    )(
        tokens.reshape((heads + 2) * CH, 4 * MEL),
        weights,
        bias_rows,
        gain_row,
        position_bias,
        pltpu.with_memory_space_constraint(jnp.transpose(qkv_weight, (1, 0, 2)), pltpu.HBM),
        pltpu.with_memory_space_constraint(utt_lengths, pltpu.HBM),
    )


def solution(mesh):
    placed = (
        P(("groups", "seq"), "head", "sub", None, None),
        P(("groups", "seq"), "head", "sub", None),
        P("groups"),
        P(None, "head"),
        P("head"),
        P(),
        P(None, None, "head"),
        P("head", None),
    )
    return jax.shard_map(
        functools.partial(local, mesh.shape["seq"], mesh.shape["head"], mesh.shape["sub"]),
        mesh=mesh,
        in_specs=placed,
        out_specs=P(("groups", "seq", "sub"), "head"),
        check_vma=False,
    )
```
